32 devices in a mesh: region: 8 (over z, x), band: 4 (over y, core).
Axes of the slice: x: 2, y: 2, z: 4, core: 2. Of those that a mesh axis runs over, the one named last changes fastest.
Arguments:
- probes: bfloat16 [4, 4, 512, 8192], P(None, None, 'band', 'region'), may hold values from -5 to 5
- filter_taps: float32 [2, 2, 17], replicated, may hold values from 0.02 to 1
- mixing: float32 [2, 4, 4], replicated, as said below
- nugget: float32 [4], replicated, may hold values from 0.3 to 1.5
- land_span: int32 [2, 512, 8], P(None, 'band', 'region'), may hold values from 0 to 1024, as said below
Outputs:
- covariance_probes: bfloat16 [4, 4, 512, 8192], P(None, None, 'band', 'region')
- quadratic: float32 [4, 3], replicated
The draws below stay inside these ranges and needn't reach their ends.
Inputs may be any that keep to these rules, and one draw needn't show every extreme that they name: Row r of region block b has land in the columns land_span[0, r, b] to land_span[1, r, b] - 1 of the block; land_span[0] <= land_span[1] everywhere. `mixing`: each of the 2 matrices is symmetric positive definite.
All inputs are finite; a program needn't handle non-finite values.
Results may differ from the reference program's by a relative error of at most 0.0062.
Values may be sent and summed in bfloat16 or wider, within the bound.
No kernel may reach another device: no remote copies, remote signals or barrier semaphores. Data moves between devices by JAX's collectives and lax.ppermute only.
A program may use at most 128 MiB of HBM per device.

```python
import math
import jax
import jax.numpy as jnp
from jax import lax

PROBES = 4
VARS = 4
KERNELS = 2
HALF = 16
COLS_DEV = 1024
NY = 512
NX = 8192
N_REGION = 8


def draw_mixing(key, part):
    factor = jax.random.normal(jax.random.fold_in(key, 11), (KERNELS, VARS, VARS), jnp.float32) * 0.5
    return jnp.einsum('kvr,kwr->kvw', factor, factor) + 0.3 * jnp.eye(VARS, dtype=jnp.float32)[None]


def draw_land_span(key, part):
    region = jnp.arange(N_REGION, dtype=jnp.int32)
    base = jax.random.randint(jax.random.fold_in(key, 21), (N_REGION,), COLS_DEV // 4, COLS_DEV + 1)
    base = base * (N_REGION + 2 * region) // (3 * N_REGION - 2)
    jitter = jax.random.randint(jax.random.fold_in(key, 24), (NY, N_REGION), -16, 17)
    extent = jnp.clip(base[None, :] + jitter, 0, COLS_DEV)
    anchor = jax.random.randint(jax.random.fold_in(key, 27), (NY, N_REGION), 0, 2)
    lower = jnp.where(anchor == 1, COLS_DEV - extent, 0)
    upper = jnp.where(anchor == 1, COLS_DEV, extent)
    row = jnp.arange(NY, dtype=jnp.int32)[:, None]
    east_row = jax.random.randint(jax.random.fold_in(key, 25), (N_REGION,), 0, NY)
    west_row = jax.random.randint(jax.random.fold_in(key, 26), (N_REGION,), 0, NY)
    lower = jnp.where(row == east_row[None, :], COLS_DEV, lower)
    upper = jnp.where(row == east_row[None, :], COLS_DEV, upper)
    lower = jnp.where(row == west_row[None, :], 0, lower)
    upper = jnp.where(row == west_row[None, :], 0, upper)
    return jnp.stack([lower, upper]).astype(jnp.int32)


def block_levels(own_key, shape, pieces, least, high):
    def one(dim, shards_of):
        draws = jax.random.uniform(jax.random.fold_in(jax.random.fold_in(own_key, 6), dim), (shards_of,), jnp.float32, least / len(pieces), high / len(pieces))
        return jnp.repeat(jnp.exp(draws), shape[dim] // shards_of).reshape((-1,) + (1,) * (len(shape) - dim - 1))

    gain = one(*pieces[0])
    for cut in pieces[1:]:
        gain = gain * one(*cut)
    return gain


def bell_draw(rng, shape, scale, limit, split=(), held_as=jnp.bfloat16):
    values = jax.random.normal(rng, shape, jnp.float32) * scale
    if len(split) > 0:
        values = block_levels(rng, shape, split, -0.22, 0.18) * values
    return jnp.clip(values, min=-limit, max=limit).astype(held_as)


def setup_inputs(seed: int = 0) -> dict:
    key_of = jax.random.split(jax.random.key(seed), 6)
    probes = bell_draw(key_of[0], (PROBES, VARS, NY, NX), 1.0, 5.0, ((2, 4), (3, 8)))
    filter_taps = jnp.clip(jnp.exp(jax.random.uniform(key_of[1], (KERNELS, 2, HALF + 1), jnp.float32, math.log(0.02), math.log(1.0))), 0.02, 1.0)
    mixing = draw_mixing(jax.random.fold_in(key_of[5], 71), 0)
    nugget = jnp.clip(jnp.exp(jax.random.uniform(key_of[3], (VARS,), jnp.float32, math.log(0.3), math.log(1.5))), 0.3, 1.5)
    land_span = draw_land_span(jax.random.fold_in(key_of[5], 71), 0)
    return dict(probes=probes, filter_taps=filter_taps, mixing=mixing, nugget=nugget, land_span=land_span)


def convolve_columns(plane, weights):
    half_width = (weights.shape[0] - 1) // 2
    count = plane.shape[1]
    padded = jnp.concatenate([plane[:, count - half_width:], plane, plane[:, :half_width]], axis=1)
    total = jnp.zeros_like(plane)
    for shift in range(weights.shape[0]):
        total = total + weights[shift] * padded[:, shift:shift + count]
    return total


def convolve_rows(plane, weights):
    half_width = (weights.shape[0] - 1) // 2
    count = plane.shape[0]
    padded = jnp.pad(plane, ((half_width, half_width), (0, 0)))
    total = jnp.zeros_like(plane)
    for shift in range(weights.shape[0]):
        total = total + weights[shift] * padded[shift:shift + count, :]
    return total


def reference(probes, filter_taps, mixing, nugget, land_span):
    rounded = lax.optimization_barrier(filter_taps.astype(jnp.bfloat16)).astype(jnp.float32)
    mirrored = jnp.concatenate([rounded[:, :, :0:-1], rounded], axis=2)
    column = jnp.arange(NX, dtype=jnp.int32)
    region_of = (column // COLS_DEV).astype(jnp.int32)
    local_col = (column % COLS_DEV).astype(jnp.int32)
    lower = land_span[0][:, region_of]
    upper = land_span[1][:, region_of]
    landed = (local_col[None, :] >= lower) & (local_col[None, :] < upper)

    def one_probe(field):
        masked = jnp.where(landed[None], field, jnp.zeros((), field.dtype)).astype(jnp.float32)
        total = nugget[:, None, None] * masked
        quad_terms = []
        for kernel in range(KERNELS):
            mixed = jnp.zeros_like(masked)
            for source in range(VARS):
                across = convolve_columns(masked[source], mirrored[kernel, 0])
                across = lax.optimization_barrier(across.astype(jnp.bfloat16)).astype(jnp.float32)
                smooth = convolve_rows(across, mirrored[kernel, 1])
                mixed = mixed + mixing[kernel, :, source][:, None, None] * smooth[None]
            quad_terms.append(jnp.sum(mixed * masked))
            total = total + mixed
        quad_terms.append(jnp.sum(nugget[:, None, None] * masked * masked))
        output = jnp.where(landed[None], total, jnp.zeros((), total.dtype)).astype(jnp.bfloat16)
        return output, jnp.stack(quad_terms) / (NY * COLS_DEV)

    outputs, quadratic = lax.map(one_probe, probes)
    return outputs, quadratic
```

```python
import functools

import jax
import jax.numpy as jnp
from jax import lax
from jax.experimental import pallas as pl
from jax.experimental.pallas import tpu as pltpu
from jax.sharding import PartitionSpec as P

LANES = 128
BF16 = jnp.bfloat16
F32 = jnp.float32


def bounds_by_row(span_ref):
    out = []
    for entry in range(2):
        line = jnp.broadcast_to(span_ref[entry].astype(F32), (LANES, LANES))
        out.append(line.T)
    return out


def land_tile(low, high, first_col):
    column = (lax.broadcasted_iota(jnp.int32, low.shape, 1) + first_col).astype(F32)
    return ((column >= low) & (column < high)).astype(F32).astype(BF16)


def pack_kernel(half, span_ref, west_ref, east_ref, top_ref, bottom_ref, left_ref, right_ref, up_ref, down_ref):
    probes, variables, rows, _ = west_ref.shape
    cols = top_ref.shape[3]
    planes = probes * variables
    per_group = LANES // half
    low, high = bounds_by_row(span_ref)
    first = land_tile(low, high, 0)
    last = land_tile(low, high, cols - LANES)
    for group in range(left_ref.shape[0]):
        heads, tails = [], []
        for plane in range(group * per_group, min(planes, (group + 1) * per_group)):
            at = (plane // variables, plane % variables)
            heads.append((west_ref[at] * first)[:, :half])
            tails.append((east_ref[at] * last)[:, LANES - half :])
        left_ref[group] = jnp.concatenate(heads, axis=1)
        right_ref[group] = jnp.concatenate(tails, axis=1)
    for tile in range(cols // LANES):
        lanes = slice(tile * LANES, (tile + 1) * LANES)
        above = land_tile(low[:half], high[:half], tile * LANES)
        below = land_tile(low[rows - half :], high[rows - half :], tile * LANES)
        up_ref[:, :, :, lanes] = top_ref[:, :, :, lanes] * above[None, None]
        down_ref[:, :, :, lanes] = bottom_ref[:, :, :, lanes] * below[None, None]


def pack(probes, span, half):
    count, variables, rows, cols = probes.shape
    groups = count * variables * half // LANES
    lead = (count, variables)
    full = lambda shape: pl.BlockSpec(shape, lambda _: (0,) * len(shape))
    edge = jax.ShapeDtypeStruct((groups, rows, LANES), BF16)
    strip = jax.ShapeDtypeStruct((*lead, half, cols), BF16)
    return pl.pallas_call(
        functools.partial(pack_kernel, half),
        grid=(1,),
        out_shape=(edge, edge, strip, strip),
        in_specs=[
            full(span.shape),
            pl.BlockSpec((*lead, rows, LANES), lambda _: (0, 0, 0, 0)),
            pl.BlockSpec((*lead, rows, LANES), lambda _: (0, 0, 0, cols // LANES - 1)),
            pl.BlockSpec((*lead, half, cols), lambda _: (0, 0, 0, 0)),
            pl.BlockSpec((*lead, half, cols), lambda _: (0, 0, rows // half - 1, 0)),
        ],
        out_specs=(full(edge.shape), full(edge.shape), full(strip.shape), full(strip.shape)),
        compiler_params=pltpu.CompilerParams(vmem_limit_bytes=24 << 20),
        name="pack",
    )(span, probes, probes, probes, probes)


def table_kernel(taps_ref, across_ref, downward_ref):
    kernels, _, count = taps_ref.shape
    half = count - 1

    def toeplitz(kernel, which, distance):
        table = jnp.zeros(distance.shape, F32)
        for tap in range(count):
            table = jnp.where(distance == tap, taps_ref[kernel, which, tap], table)
        return table.astype(BF16)

    for kernel in range(kernels):
        shape = (across_ref.shape[0], LANES)
        gap = lax.broadcasted_iota(jnp.int32, shape, 0) - lax.broadcasted_iota(jnp.int32, shape, 1)
        across_ref[:, kernel * LANES : (kernel + 1) * LANES] = toeplitz(kernel, 0, jnp.abs(gap - half))
        shape = downward_ref.shape[1:]
        gap = lax.broadcasted_iota(jnp.int32, shape, 1) - lax.broadcasted_iota(jnp.int32, shape, 0)
        downward_ref[kernel] = toeplitz(kernel, 1, jnp.abs(gap - half))


def tables(taps, rows):
    kernels, _, count = taps.shape
    return pl.pallas_call(
        table_kernel,
        out_shape=(
            jax.ShapeDtypeStruct((2 * LANES, kernels * LANES), BF16),
            jax.ShapeDtypeStruct((kernels, rows, rows + 2 * (count - 1)), BF16),
        ),
        in_specs=[pl.BlockSpec(memory_space=pltpu.SMEM)],
        name="tables",
    )(taps)


def main_kernel(
    half,
    mixing_ref,
    nugget_ref,
    span_ref,
    across_ref,
    downward_ref,
    x_ref,
    west_ref,
    east_ref,
    north_ref,
    south_ref,
    above_ref,
    below_ref,
    out_ref,
    quad_ref,
    land_ref,
    ext_ref,
    interior_ref,
    sums_ref,
):
    probe = pl.program_id(0)
    variables, rows, cols = x_ref.shape[1:]
    kernels = downward_ref.shape[0]
    tiles = cols // LANES
    tall = rows + 2 * half

    @pl.when(probe == 0)
    def _():
        low, high = bounds_by_row(span_ref)
        for tile in range(tiles):
            land_ref[:, tile * LANES : (tile + 1) * LANES] = land_tile(low, high, tile * LANES)

    groups = west_ref.shape[0]
    per_group = LANES // half // variables
    group, slot = probe // per_group, probe % per_group

    def side(ref, index):
        block = ref[index].astype(F32)
        return pltpu.roll(block, (per_group - slot) * (half * variables) % LANES, 1)

    def extend(rows_at, height, tile_of, west, east):
        lane = lax.broadcasted_iota(jnp.int32, (height, LANES), 1)
        for v in range(variables):
            back = LANES - half * v
            before = pltpu.roll(west, back % LANES, 1)
            for tile in range(tiles):
                moved = pltpu.roll(tile_of(v, tile).astype(F32), half, 1)
                ext_ref[v, rows_at : rows_at + height, tile * LANES : (tile + 1) * LANES] = jnp.where(
                    lane < half, before, moved
                ).astype(BF16)
                before = moved
            after = pltpu.roll(east, (back + half) % LANES, 1)
            final = jnp.where(lane < half, before, jnp.where(lane < 2 * half, after, 0.0))
            ext_ref[v, rows_at : rows_at + height, cols : cols + LANES] = final.astype(BF16)

    def lanes_of(tile):
        return slice(tile * LANES, (tile + 1) * LANES)

    extend(
        half,
        rows,
        lambda v, t: x_ref[0, v, :, lanes_of(t)] * land_ref[:, lanes_of(t)],
        side(west_ref, group),
        side(east_ref, group),
    )
    extend(0, half, lambda v, t: north_ref[0, v, :, lanes_of(t)], side(above_ref, group), side(above_ref, groups + group))
    extend(
        half + rows, half, lambda v, t: south_ref[0, v, :, lanes_of(t)], side(below_ref, group), side(below_ref, groups + group)
    )

    for tile in range(tiles):
        window = ext_ref[:, :, tile * LANES : (tile + 2) * LANES].reshape(variables * tall, 2 * LANES)
        both = jnp.dot(window, across_ref[...], preferred_element_type=F32).astype(BF16)
        for kernel in range(kernels):
            interior_ref[kernel, :, :, lanes_of(tile)] = both[:, lanes_of(kernel)].reshape(variables, tall, LANES)

    sums = [jnp.zeros((8, LANES), F32) for _ in range(kernels + 1)]
    wide = 2 * LANES
    for chunk in range(cols // wide):
        span = slice(chunk * wide, (chunk + 1) * wide)
        smooth = [
            [
                jnp.dot(downward_ref[kernel], interior_ref[kernel, w, :, span], preferred_element_type=F32)
                for w in range(variables)
            ]
            for kernel in range(kernels)
        ]
        land = land_ref[:, span].astype(F32)
        for v in range(variables):
            local = (x_ref[0, v, :, span] * land_ref[:, span]).astype(F32)
            total = nugget_ref[v] * local
            parts = [total * local]
            for kernel in range(kernels):
                term = mixing_ref[kernel, v, 0] * smooth[kernel][0]
                for w in range(1, variables):
                    term = term + mixing_ref[kernel, v, w] * smooth[kernel][w]
                parts.append(term * local)
                total = total + term
            out_ref[0, v, :, span] = (total * land).astype(BF16)
            for k, part in enumerate(parts[1:] + parts[:1]):
                folded = jnp.sum(part.reshape(rows // 8, 8, wide), axis=0)
                sums[k] = sums[k] + folded[:, :LANES] + folded[:, LANES:]
    for k in range(kernels + 1):
        sums_ref[probe, k] = sums[k]

    @pl.when(probe == pl.num_programs(0) - 1)
    def _():
        lane = lax.broadcasted_iota(jnp.int32, quad_ref.shape, 1)
        line = jnp.zeros(quad_ref.shape, F32)
        for p in range(sums_ref.shape[0]):
            for k in range(kernels + 1):
                line = jnp.where(lane == p * (kernels + 1) + k, jnp.sum(sums_ref[p, k]), line)
        quad_ref[...] = line


def main(mixing, nugget, span, across, downward, probes, west, east, north, south, above, below, half, devices):
    count, variables, rows, cols = probes.shape
    kernels = downward.shape[0]
    tall = rows + 2 * half
    full = lambda a: pl.BlockSpec(a.shape, lambda p: (0,) * a.ndim)
    one = lambda height: pl.BlockSpec((1, variables, height, cols), lambda p: (p, 0, 0, 0))
    smem = pl.BlockSpec(memory_space=pltpu.SMEM)
    return pl.pallas_call(
        functools.partial(main_kernel, half),
        grid=(count,),
        out_shape=(jax.ShapeDtypeStruct(probes.shape, BF16), jax.ShapeDtypeStruct((devices, LANES), F32)),
        in_specs=[
            smem,
            smem,
            full(span),
            full(across),
            full(downward),
            one(rows),
            full(west),
            full(east),
            one(half),
            one(half),
            full(above),
            full(below),
        ],
        out_specs=(one(rows), pl.BlockSpec((devices, LANES), lambda p: (0, 0))),
        scratch_shapes=[
            pltpu.VMEM((rows, cols), BF16),
            pltpu.VMEM((variables, tall, cols + LANES), BF16),
            pltpu.VMEM((kernels, variables, tall, cols), BF16),
            pltpu.VMEM((count, kernels + 1, 8, LANES), F32),
        ],
        compiler_params=pltpu.CompilerParams(vmem_limit_bytes=40 << 20),
        name="covariance",
    )(mixing, nugget, span, across, downward, probes, west, east, north, south, above, below)


def per_device(probes, filter_taps, mixing, nugget, land_span):
    count, variables, rows, cols = probes.shape
    kernels = filter_taps.shape[0]
    half = filter_taps.shape[2] - 1
    regions, bands = lax.axis_size("region"), lax.axis_size("band")
    east_of = [(i, (i + 1) % regions) for i in range(regions)]
    west_of = [((i + 1) % regions, i) for i in range(regions)]
    south_of = [(i, i + 1) for i in range(bands - 1)]
    north_of = [(i + 1, i) for i in range(bands - 1)]

    span = land_span.reshape(2, 1, rows)
    left, right, up, down = pack(probes, span, half)
    west = lax.ppermute(right, "region", east_of)
    east = lax.ppermute(left, "region", west_of)
    north = lax.ppermute(down, "band", south_of)
    south = lax.ppermute(up, "band", north_of)
    across, downward = tables(filter_taps, rows)
    above = lax.ppermute(jnp.concatenate([west[:, rows - half :], east[:, rows - half :]]), "band", south_of)
    below = lax.ppermute(jnp.concatenate([west[:, :half], east[:, :half]]), "band", north_of)
    output, quads = main(
        mixing, nugget, span, across, downward, probes, west, east, north, south, above, below, half, regions * bands
    )
    shares = lax.all_to_all(quads, ("region", "band"), 0, 0, tiled=True)
    quadratic = jnp.sum(shares, axis=0)[: count * (kernels + 1)].reshape(count, kernels + 1)
    return output, quadratic / (bands * rows * cols)


def solution(mesh):
    in_specs = (P(None, None, "band", "region"), P(), P(), P(), P(None, "band", "region"))
    out_specs = (P(None, None, "band", "region"), P())
    return jax.shard_map(
        per_device, mesh=mesh, in_specs=in_specs, out_specs=out_specs, check_vma=False
    )
```

```python
import functools

import jax
import jax.numpy as jnp
from jax import lax
from jax.experimental import pallas as pl
from jax.experimental.pallas import tpu as pltpu
from jax.sharding import PartitionSpec as P

LANES = 128
BF16 = jnp.bfloat16
F32 = jnp.float32
VMEM = 61 << 20


def bounds_by_row(span_ref):
    out = []
    for entry in range(2):
        line = jnp.broadcast_to(span_ref[entry].astype(F32), (LANES, LANES))
        out.append(line.T)
    return out


def land_tile(low, high, first_col):
    column = (lax.broadcasted_iota(jnp.int32, low.shape, 1) + first_col).astype(F32)
    return ((column >= low) & (column < high)).astype(F32).astype(BF16)


def pack_kernel(
    half, odd_ref, span_ref, west_ref, east_ref, top_ref, bottom_ref, inner_ref, outer_ref, near_ref, far_ref
):
    probes, variables, rows, _ = west_ref.shape
    cols = top_ref.shape[3]
    planes = probes * variables
    per_group = LANES // half
    low, high = bounds_by_row(span_ref)
    first = land_tile(low, high, 0)
    last = land_tile(low, high, cols - LANES)

    def columns(left_ref, right_ref):
        for group in range(left_ref.shape[0]):
            heads, tails = [], []
            for plane in range(group * per_group, min(planes, (group + 1) * per_group)):
                at = (plane // variables, plane % variables)
                heads.append((west_ref[at] * first)[:, :half])
                tails.append((east_ref[at] * last)[:, LANES - half :])
            left_ref[group] = jnp.concatenate(heads, axis=1)
            right_ref[group] = jnp.concatenate(tails, axis=1)

    def strips(up_ref, down_ref):
        for tile in range(cols // LANES):
            lanes = slice(tile * LANES, (tile + 1) * LANES)
            above = land_tile(low[:half], high[:half], tile * LANES)
            below = land_tile(low[rows - half :], high[rows - half :], tile * LANES)
            up_ref[:, :, :, lanes] = top_ref[:, :, :, lanes] * above[None, None]
            down_ref[:, :, :, lanes] = bottom_ref[:, :, :, lanes] * below[None, None]

    for which, work, ends in ((0, columns, (outer_ref, inner_ref)), (1, strips, (far_ref, near_ref))):

        @pl.when(odd_ref[which] == 0)
        def _(work=work, ends=ends):
            work(*ends)

        @pl.when(odd_ref[which] != 0)
        def _(work=work, ends=ends):
            work(*ends[::-1])


def pack(odd, probes, span, half):
    count, variables, rows, cols = probes.shape
    groups = count * variables * half // LANES
    lead = (count, variables)
    full = lambda shape: pl.BlockSpec(shape, lambda _: (0,) * len(shape))
    edge = jax.ShapeDtypeStruct((groups, rows, LANES), BF16)
    strip = jax.ShapeDtypeStruct((*lead, half, cols), BF16)
    return pl.pallas_call(
        functools.partial(pack_kernel, half),
        grid=(1,),
        out_shape=(edge, edge, strip, strip),
        in_specs=[
            pl.BlockSpec(memory_space=pltpu.SMEM),
            full(span.shape),
            pl.BlockSpec((*lead, rows, LANES), lambda _: (0, 0, 0, 0)),
            pl.BlockSpec((*lead, rows, LANES), lambda _: (0, 0, 0, cols // LANES - 1)),
            pl.BlockSpec((*lead, half, cols), lambda _: (0, 0, 0, 0)),
            pl.BlockSpec((*lead, half, cols), lambda _: (0, 0, rows // half - 1, 0)),
        ],
        out_specs=(full(edge.shape), full(edge.shape), full(strip.shape), full(strip.shape)),
        compiler_params=pltpu.CompilerParams(vmem_limit_bytes=VMEM),
        name="pack",
    )(odd, span, probes, probes, probes, probes)


def table_kernel(taps_ref, across_ref, downward_ref):
    kernels, _, count = taps_ref.shape
    half = count - 1

    def toeplitz(kernel, which, distance):
        table = jnp.zeros(distance.shape, F32)
        for tap in range(count):
            table = jnp.where(distance == tap, taps_ref[kernel, which, tap], table)
        return table.astype(BF16)

    for kernel in range(kernels):
        shape = (across_ref.shape[0], LANES)
        gap = lax.broadcasted_iota(jnp.int32, shape, 0) - lax.broadcasted_iota(jnp.int32, shape, 1)
        across_ref[:, kernel * LANES : (kernel + 1) * LANES] = toeplitz(kernel, 0, jnp.abs(gap - half))
        shape = downward_ref.shape[1:]
        gap = lax.broadcasted_iota(jnp.int32, shape, 1) - lax.broadcasted_iota(jnp.int32, shape, 0)
        downward_ref[kernel] = toeplitz(kernel, 1, jnp.abs(gap - half))


def tables(taps, rows):
    kernels, _, count = taps.shape
    return pl.pallas_call(
        table_kernel,
        out_shape=(
            jax.ShapeDtypeStruct((2 * LANES, kernels * LANES), BF16),
            jax.ShapeDtypeStruct((kernels, rows, rows + 2 * (count - 1)), BF16),
        ),
        in_specs=[pl.BlockSpec(memory_space=pltpu.SMEM)],
        name="tables",
    )(taps)


def main_kernel(
    half,
    odd_ref,
    mixing_ref,
    nugget_ref,
    span_ref,
    across_ref,
    downward_ref,
    x_ref,
    inner_ref,
    outer_ref,
    near_ref,
    far_ref,
    near_corner_ref,
    far_corner_ref,
    out_ref,
    quad_ref,
    land_ref,
    ext_ref,
    interior_ref,
    sums_ref,
):
    probe = pl.program_id(0)
    variables, rows, cols = x_ref.shape[1:]
    kernels = downward_ref.shape[0]
    tiles = cols // LANES
    tall = rows + 2 * half

    @pl.when(probe == 0)
    def _():
        low, high = bounds_by_row(span_ref)
        for tile in range(tiles):
            land_ref[:, tile * LANES : (tile + 1) * LANES] = land_tile(low, high, tile * LANES)

    groups = inner_ref.shape[0]
    per_group = LANES // half // variables
    group, slot = probe // per_group, probe % per_group
    odd_region, odd_band = odd_ref[0] != 0, odd_ref[1] != 0

    def side(block):
        return pltpu.roll(block.astype(F32), (per_group - slot) * (half * variables) % LANES, 1)

    def sides(inner, outer):
        return side(jnp.where(odd_region, inner, outer)), side(jnp.where(odd_region, outer, inner))

    def extend(rows_at, height, tile_of, west, east):
        lane = lax.broadcasted_iota(jnp.int32, (height, LANES), 1)
        for v in range(variables):
            back = LANES - half * v
            before = pltpu.roll(west, back % LANES, 1)
            for tile in range(tiles):
                moved = pltpu.roll(tile_of(v, tile).astype(F32), half, 1)
                ext_ref[v, rows_at : rows_at + height, tile * LANES : (tile + 1) * LANES] = jnp.where(
                    lane < half, before, moved
                ).astype(BF16)
                before = moved
            after = pltpu.roll(east, (back + half) % LANES, 1)
            final = jnp.where(lane < half, before, jnp.where(lane < 2 * half, after, 0.0))
            ext_ref[v, rows_at : rows_at + height, cols : cols + LANES] = final.astype(BF16)

    def lanes_of(tile):
        return slice(tile * LANES, (tile + 1) * LANES)

    extend(
        half,
        rows,
        lambda v, t: x_ref[0, v, :, lanes_of(t)] * land_ref[:, lanes_of(t)],
        *sides(inner_ref[group], outer_ref[group]),
    )
    for rows_at, from_near in ((0, odd_band), (half + rows, jnp.logical_not(odd_band))):
        corner = [
            jnp.where(from_near, near_corner_ref[kind + group], far_corner_ref[kind + group]) for kind in (0, groups)
        ]
        extend(
            rows_at,
            half,
            lambda v, t, near=from_near: jnp.where(near, near_ref[0, v, :, lanes_of(t)], far_ref[0, v, :, lanes_of(t)]),
            *sides(*corner),
        )

    for tile in range(tiles):
        window = ext_ref[:, :, tile * LANES : (tile + 2) * LANES].reshape(variables * tall, 2 * LANES)
        both = jnp.dot(window, across_ref[...], preferred_element_type=F32).astype(BF16)
        for kernel in range(kernels):
            interior_ref[kernel, :, :, lanes_of(tile)] = both[:, lanes_of(kernel)].reshape(variables, tall, LANES)

    sums = [jnp.zeros((8, LANES), F32) for _ in range(kernels + 1)]
    wide = 2 * LANES
    for chunk in range(cols // wide):
        span = slice(chunk * wide, (chunk + 1) * wide)
        smooth = [
            [
                jnp.dot(downward_ref[kernel], interior_ref[kernel, w, :, span], preferred_element_type=F32)
                for w in range(variables)
            ]
            for kernel in range(kernels)
        ]
        land = land_ref[:, span].astype(F32)
        for v in range(variables):
            local = (x_ref[0, v, :, span] * land_ref[:, span]).astype(F32)
            total = nugget_ref[v] * local
            parts = [total * local]
            for kernel in range(kernels):
                term = mixing_ref[kernel, v, 0] * smooth[kernel][0]
                for w in range(1, variables):
                    term = term + mixing_ref[kernel, v, w] * smooth[kernel][w]
                parts.append(term * local)
                total = total + term
            out_ref[0, v, :, span] = (total * land).astype(BF16)
            for k, part in enumerate(parts[1:] + parts[:1]):
                folded = jnp.sum(part.reshape(rows // 8, 8, wide), axis=0)
                sums[k] = sums[k] + folded[:, :LANES] + folded[:, LANES:]
    for k in range(kernels + 1):
        sums_ref[probe, k] = sums[k]

    @pl.when(probe == pl.num_programs(0) - 1)
    def _():
        lane = lax.broadcasted_iota(jnp.int32, quad_ref.shape, 1)
        line = jnp.zeros(quad_ref.shape, F32)
        for p in range(sums_ref.shape[0]):
            for k in range(kernels + 1):
                line = jnp.where(lane == p * (kernels + 1) + k, jnp.sum(sums_ref[p, k]), line)
        quad_ref[...] = line


def main(odd, mixing, nugget, span, across, downward, probes, inner, outer, near, far, near_corner, far_corner, half, devices):
    count, variables, rows, cols = probes.shape
    kernels = downward.shape[0]
    tall = rows + 2 * half
    full = lambda a: pl.BlockSpec(a.shape, lambda p: (0,) * a.ndim)
    one = lambda height: pl.BlockSpec((1, variables, height, cols), lambda p: (p, 0, 0, 0))
    smem = pl.BlockSpec(memory_space=pltpu.SMEM)
    return pl.pallas_call(
        functools.partial(main_kernel, half),
        grid=(count,),
        out_shape=(jax.ShapeDtypeStruct(probes.shape, BF16), jax.ShapeDtypeStruct((devices, LANES), F32)),
        in_specs=[
            smem,
            smem,
            smem,
            full(span),
            full(across),
            full(downward),
            one(rows),
            full(inner),
            full(outer),
            one(half),
            one(half),
            full(near_corner),
            full(far_corner),
        ],
        out_specs=(one(rows), pl.BlockSpec((devices, LANES), lambda p: (0, 0))),
        scratch_shapes=[
            pltpu.VMEM((rows, cols), BF16),
            pltpu.VMEM((variables, tall, cols + LANES), BF16),
            pltpu.VMEM((kernels, variables, tall, cols), BF16),
            pltpu.VMEM((count, kernels + 1, 8, LANES), F32),
        ],
        compiler_params=pltpu.CompilerParams(vmem_limit_bytes=VMEM),
        name="covariance",
    )(odd, mixing, nugget, span, across, downward, probes, inner, outer, near, far, near_corner, far_corner)


def per_device(probes, filter_taps, mixing, nugget, land_span):
    count, variables, rows, cols = probes.shape
    kernels = filter_taps.shape[0]
    half = filter_taps.shape[2] - 1
    regions, bands = lax.axis_size("region"), lax.axis_size("band")
    pairs = {
        "inner": [(i, i ^ 1) for i in range(regions)],
        "outer": [(i, (i + 1 if i % 2 else i - 1) % regions) for i in range(regions)],
        "near": [(i, i ^ 1) for i in range(bands)],
        "far": [(i, i + 1 if i % 2 else i - 1) for i in range(1, bands - 1)],
    }

    odd = jnp.stack([lax.axis_index("region") % 2, lax.axis_index("band") % 2]).astype(jnp.int32)
    span = land_span.reshape(2, 1, rows)
    inner, outer, near, far = pack(odd, probes, span, half)
    inner = lax.ppermute(inner, "region", pairs["inner"])
    outer = lax.ppermute(outer, "region", pairs["outer"])
    near = lax.ppermute(near, "band", pairs["near"])
    far = lax.ppermute(far, "band", pairs["far"])
    across, downward = tables(filter_taps, rows)
    top = jnp.concatenate([inner[:, :half], outer[:, :half]])
    bottom = jnp.concatenate([inner[:, rows - half :], outer[:, rows - half :]])
    near_corner = lax.ppermute(jnp.where(odd[1] != 0, top, bottom), "band", pairs["near"])
    far_corner = lax.ppermute(jnp.where(odd[1] != 0, bottom, top), "band", pairs["far"])
    output, quads = main(
        odd,
        mixing,
        nugget,
        span,
        across,
        downward,
        probes,
        inner,
        outer,
        near,
        far,
        near_corner,
        far_corner,
        half,
        regions * bands,
    )
    shares = lax.all_to_all(quads, ("region", "band"), 0, 0, tiled=True)
    quadratic = jnp.sum(shares, axis=0)[: count * (kernels + 1)].reshape(count, kernels + 1)
    return output, quadratic / (bands * rows * cols)


def solution(mesh):
    in_specs = (P(None, None, "band", "region"), P(), P(), P(), P(None, "band", "region"))
    out_specs = (P(None, None, "band", "region"), P())
    return jax.shard_map(
        per_device, mesh=mesh, in_specs=in_specs, out_specs=out_specs, check_vma=False
    )
```

```python
import functools

import jax
import jax.numpy as jnp
from jax import lax
from jax.experimental import pallas as pl
from jax.experimental.pallas import tpu as pltpu
from jax.sharding import PartitionSpec as P

LANES = 128
BF16 = jnp.bfloat16
F32 = jnp.float32
SMEM = pl.BlockSpec(memory_space=pltpu.SMEM)


def lanes_of(tile):
    return slice(tile * LANES, (tile + 1) * LANES)


def whole(a):
    return pl.BlockSpec(a.shape, lambda *_: (0,) * len(a.shape))


def odd(axis):
    return lax.axis_index(axis) % 2 != 0


def bounds_by_row(span_ref):
    return [jnp.broadcast_to(span_ref[entry].astype(F32), (LANES, LANES)).T for entry in range(2)]


def land_tile(low, high, first_col):
    column = (lax.broadcasted_iota(jnp.int32, low.shape, 1) + first_col).astype(F32)
    return ((column >= low) & (column < high)).astype(F32).astype(BF16)


def pack_kernel(half, cols, span_ref, west_ref, east_ref, inner_ref, outer_ref):
    probes, variables, _, _ = west_ref.shape
    per_group = LANES // half
    low, high = bounds_by_row(span_ref)
    first = land_tile(low, high, 0)
    last = land_tile(low, high, cols - LANES)
    swapped = odd("region")
    for group in range(inner_ref.shape[0]):
        heads, tails = [], []
        for plane in range(group * per_group, (group + 1) * per_group):
            at = (plane // variables, plane % variables)
            heads.append((west_ref[at] * first)[:, :half])
            tails.append((east_ref[at] * last)[:, LANES - half :])
        left, right = jnp.concatenate(heads, axis=1), jnp.concatenate(tails, axis=1)
        inner_ref[group] = jnp.where(swapped, left, right)
        outer_ref[group] = jnp.where(swapped, right, left)


def pack(probes, span, half):
    count, variables, rows, cols = probes.shape
    edge = jax.ShapeDtypeStruct((count * variables * half // LANES, rows, LANES), BF16)
    tile = lambda at: pl.BlockSpec((count, variables, rows, LANES), lambda _: (0, 0, 0, at))
    kernel = functools.partial(pack_kernel, half, cols)
    return pl.pallas_call(
        kernel,
        grid=(1,),
        out_shape=(edge, edge),
        in_specs=[whole(span), tile(0), tile(cols // LANES - 1)],
        out_specs=(whole(edge), whole(edge)),
        compiler_params=pltpu.CompilerParams(vmem_limit_bytes=16 << 20),
        name="pack",
    )(span, probes, probes)


def prepare_kernel(
    half,
    taps_ref,
    mixing_ref,
    span_ref,
    top_ref,
    bottom_ref,
    near_ref,
    far_ref,
    shore_ref,
    across_ref,
    downward_ref,
    fringe_ref,
):
    probes, variables, _, cols = top_ref.shape
    kernels = downward_ref.shape[0]
    swapped = odd("band")
    low, high = bounds_by_row(span_ref)
    for tile in range(cols // LANES):
        lanes = lanes_of(tile)
        above = land_tile(low[:half], high[:half], tile * LANES)
        below = land_tile(low[-half:], high[-half:], tile * LANES)
        shore_ref[0, :, lanes] = above
        shore_ref[1, :, lanes] = below
        for plane in range(probes * variables):
            at = (plane // variables, plane % variables, slice(None), lanes)
            up, down = top_ref[at] * above, bottom_ref[at] * below
            near_ref[plane, :, lanes] = jnp.where(swapped, up, down)
            far_ref[plane, :, lanes] = jnp.where(swapped, down, up)

    def filtered(kernel, which, distance):
        table = jnp.zeros(distance.shape, F32)
        for tap in range(half + 1):
            table = jnp.where(distance == tap, taps_ref[kernel, which, tap], table)
        return table.astype(BF16)

    def places(shape):
        return lax.broadcasted_iota(jnp.int32, shape, 0), lax.broadcasted_iota(jnp.int32, shape, 1)

    for kernel in range(kernels):
        row, column = places((across_ref.shape[0], LANES))
        across_ref[:, lanes_of(kernel)] = filtered(kernel, 0, jnp.abs(row - column - half))
        row, column = places(downward_ref.shape[1:])
        downward_ref[kernel] = filtered(kernel, 1, jnp.abs(row - column))
        size = fringe_ref.shape[1]
        row, column = places((size, size))
        bits = half.bit_length() - 1
        i, h = row & (half - 1), column & (half - 1)
        side = (row >> bits) & 1
        gap = jnp.where(side == 0, i - h, h - i)
        reach = (gap <= 0) & (side == ((column >> bits) & 1))
        weight = filtered(kernel, 1, jnp.where(reach, gap + half, -1)).astype(F32)
        v, w = row >> (bits + 1), column >> (bits + 1)
        mixed = jnp.zeros((size, size), F32)
        for a in range(variables):
            for b in range(variables):
                mixed = jnp.where((v == a) & (w == b), mixing_ref[kernel, a, b], mixed)
        weight = weight * mixed
        coarse = weight.astype(BF16)
        fringe_ref[kernel, :, :size] = coarse
        fringe_ref[kernel, :, size:] = (weight - coarse.astype(F32)).astype(BF16)


def prepare(probes, taps, mixing, span, half):
    count, variables, rows, cols = probes.shape
    kernels = taps.shape[0]
    size = 2 * half * variables
    strip = jax.ShapeDtypeStruct((count * variables + 1, half, cols), BF16)
    outs = (
        strip,
        strip,
        jax.ShapeDtypeStruct((2, half, cols), BF16),
        jax.ShapeDtypeStruct((2 * LANES, kernels * LANES), BF16),
        jax.ShapeDtypeStruct((kernels, rows, rows), BF16),
        jax.ShapeDtypeStruct((kernels, size, 2 * size), BF16),
    )
    edge = lambda at: pl.BlockSpec((count, variables, half, cols), lambda _: (0, 0, at, 0))
    return pl.pallas_call(
        functools.partial(prepare_kernel, half),
        grid=(1,),
        out_shape=outs,
        in_specs=[SMEM, SMEM, whole(span), edge(0), edge(rows // half - 1)],
        out_specs=tuple(whole(o) for o in outs),
        cost_estimate=pl.CostEstimate(flops=10**7, bytes_accessed=4 << 20, transcendentals=0),
        compiler_params=pltpu.CompilerParams(vmem_limit_bytes=16 << 20),
        name="prepare",
    )(taps, mixing, span, probes, probes)


def corner_kernel(inner_ref, outer_ref, near_in, far_in, near_ref, far_ref):
    half = near_ref.shape[1]
    groups, rows, _ = inner_ref.shape
    swapped = odd("band")
    for at, ref in ((0, inner_ref), (groups, outer_ref)):
        for group in range(groups):
            up, down = ref[group, :half], ref[group, rows - half :]
            near_ref[0, :, lanes_of(at + group)] = jnp.where(swapped, up, down)
            far_ref[0, :, lanes_of(at + group)] = jnp.where(swapped, down, up)
    rest = slice(2 * groups * LANES, near_ref.shape[2])
    near_ref[0, :, rest] = jnp.zeros_like(near_ref[0, :, rest])
    far_ref[0, :, rest] = jnp.zeros_like(far_ref[0, :, rest])


def corner(inner, outer, near, far):
    last = pl.BlockSpec((1, *near.shape[1:]), lambda _: (near.shape[0] - 1, 0, 0))
    keep = pl.BlockSpec(memory_space=pl.ANY)
    return pl.pallas_call(
        corner_kernel,
        grid=(1,),
        out_shape=(jax.ShapeDtypeStruct(near.shape, BF16),) * 2,
        in_specs=[whole(inner), whole(outer), keep, keep],
        out_specs=(last, last),
        input_output_aliases={2: 0, 3: 1},
        compiler_params=pltpu.CompilerParams(vmem_limit_bytes=16 << 20),
        name="corner",
    )(inner, outer, near, far)


def side(block, probe, half, variables):
    per_group = LANES // half // variables
    return pltpu.roll(block.astype(F32), (per_group - probe % per_group) * (half * variables) % LANES, 1)


def extend(put, height, half, variables, tiles, tile_of, west, east):
    lane = lax.broadcasted_iota(jnp.int32, (height, LANES), 1)
    for v in range(variables):
        back = LANES - half * v
        before = pltpu.roll(west, back % LANES, 1)
        for tile in range(tiles):
            moved = pltpu.roll(tile_of(v, tile).astype(F32), half, 1)
            put(v, tile, jnp.where(lane < half, before, moved).astype(BF16))
            before = moved
        after = pltpu.roll(east, (back + half) % LANES, 1)
        final = jnp.where(lane < half, before, jnp.where(lane < 2 * half, after, 0.0))
        put(v, tiles, final.astype(BF16))


def fold(part):
    height, width = part.shape
    folded = jnp.sum(part.reshape(height // 8, 8, width), axis=0)
    return sum(folded[:, lanes_of(t)] for t in range(width // LANES))


def own_kernel(
    half,
    mixing_ref,
    nugget_ref,
    span_ref,
    across_ref,
    downward_ref,
    x_ref,
    inner_ref,
    outer_ref,
    out_ref,
    edge_ref,
    sums_ref,
    land_ref,
    ext_ref,
    interior_ref,
):
    probe = pl.program_id(0)
    variables, rows, cols = x_ref.shape[1:]
    kernels = downward_ref.shape[0]
    tiles = cols // LANES

    @pl.when(probe == 0)
    def _():
        low, high = bounds_by_row(span_ref)
        for tile in range(tiles):
            land_ref[:, lanes_of(tile)] = land_tile(low, high, tile * LANES)

    group = probe // (LANES // half // variables)
    swapped = odd("region")
    inner, outer = inner_ref[group], outer_ref[group]

    def put(v, tile, value):
        ext_ref[v, :, lanes_of(tile)] = value

    extend(
        put,
        rows,
        half,
        variables,
        tiles,
        lambda v, t: x_ref[0, v, :, lanes_of(t)] * land_ref[:, lanes_of(t)],
        side(jnp.where(swapped, inner, outer), probe, half, variables),
        side(jnp.where(swapped, outer, inner), probe, half, variables),
    )
    for tile in range(tiles):
        window = ext_ref[:, :, tile * LANES : (tile + 2) * LANES].reshape(variables * rows, 2 * LANES)
        both = jnp.dot(window, across_ref[...], preferred_element_type=F32).astype(BF16)
        for kernel in range(kernels):
            interior_ref[kernel, :, :, lanes_of(tile)] = both[:, lanes_of(kernel)].reshape(variables, rows, LANES)

    sums = [jnp.zeros((8, LANES), F32) for _ in range(kernels + 1)]
    wide = 2 * LANES
    for chunk in range(cols // wide):
        span = slice(chunk * wide, (chunk + 1) * wide)
        smooth = [
            [
                jnp.dot(downward_ref[kernel], interior_ref[kernel, w, :, span], preferred_element_type=F32)
                for w in range(variables)
            ]
            for kernel in range(kernels)
        ]
        land = land_ref[:, span].astype(F32)
        for v in range(variables):
            local = (x_ref[0, v, :, span] * land_ref[:, span]).astype(F32)
            total = nugget_ref[v] * local
            parts = [total * local]
            for kernel in range(kernels):
                term = mixing_ref[kernel, v, 0] * smooth[kernel][0]
                for w in range(1, variables):
                    term = term + mixing_ref[kernel, v, w] * smooth[kernel][w]
                parts.append(term * local)
                total = total + term
            out_ref[0, v, :, span] = (total * land).astype(BF16)
            edge_ref[0, v, 0, :, span] = total[:half]
            edge_ref[0, v, 1, :, span] = total[rows - half :]
            for k, part in enumerate(parts[1:] + parts[:1]):
                sums[k] = sums[k] + fold(part)
    for k in range(kernels + 1):
        sums_ref[0, k] = sums[k]


def own(mixing, nugget, span, across, downward, probes, inner, outer, half):
    count, variables, rows, cols = probes.shape
    kernels = downward.shape[0]
    block = lambda *shape: pl.BlockSpec((1, *shape), lambda p: (p,) + (0,) * len(shape))
    outs = (
        jax.ShapeDtypeStruct(probes.shape, BF16),
        jax.ShapeDtypeStruct((count, variables, 2, half, cols), F32),
        jax.ShapeDtypeStruct((count, kernels + 1, 8, LANES), F32),
    )
    return pl.pallas_call(
        functools.partial(own_kernel, half),
        grid=(count,),
        out_shape=outs,
        in_specs=[
            SMEM,
            SMEM,
            whole(span),
            whole(across),
            whole(downward),
            block(*probes.shape[1:]),
            whole(inner),
            whole(outer),
        ],
        out_specs=tuple(block(*o.shape[1:]) for o in outs),
        scratch_shapes=[
            pltpu.VMEM((rows, cols), BF16),
            pltpu.VMEM((variables, rows, cols + LANES), BF16),
            pltpu.VMEM((kernels, variables, rows, cols), BF16),
        ],
        cost_estimate=pl.CostEstimate(flops=10**10, bytes_accessed=16 << 20, transcendentals=0),
        compiler_params=pltpu.CompilerParams(vmem_limit_bytes=32 << 20),
        name="own",
    )(mixing, nugget, span, across, downward, probes, inner, outer)


def border_kernel(
    half,
    across_ref,
    fringe_ref,
    shore_ref,
    near_ref,
    far_ref,
    near_corner_ref,
    far_corner_ref,
    near_own_ref,
    far_own_ref,
    edge_ref,
    sums_ref,
    base_ref,
    out_ref,
    quad_ref,
    ext_ref,
    ready_ref,
    total_ref,
    sem,
):
    probe = pl.program_id(0)
    variables, _, cols = near_ref.shape
    rows = out_ref.shape[2]
    count, shares = sums_ref.shape[:2]
    kernels = shares - 1
    tiles = cols // LANES
    group = probe // (LANES // half // variables)
    groups = count * variables * half // LANES
    swapped, flipped = odd("band"), odd("region")
    size = 2 * half * variables

    for at in range(2):
        from_near = swapped if at == 0 else jnp.logical_not(swapped)
        corners = []
        for kind in (0, groups):
            where = pl.ds(pl.multiple_of((kind + group) * LANES, LANES), LANES)
            corners.append(jnp.where(from_near, near_corner_ref[0, :, where], far_corner_ref[0, :, where]))
        inner, outer = corners

        def put(v, tile, value, at=at):
            first = (2 * v + at) * half
            ext_ref[first : first + half, lanes_of(tile)] = value

        extend(
            put,
            half,
            half,
            variables,
            tiles,
            lambda v, t, n=from_near: jnp.where(n, near_ref[v, :, lanes_of(t)], far_ref[v, :, lanes_of(t)]),
            side(jnp.where(flipped, inner, outer), probe, half, variables),
            side(jnp.where(flipped, outer, inner), probe, half, variables),
        )

    for tile in range(tiles):
        both = jnp.dot(
            ext_ref[:, tile * LANES : (tile + 2) * LANES], across_ref[...], preferred_element_type=F32
        ).astype(BF16)
        for kernel in range(kernels):
            piece = both[:, lanes_of(kernel)]
            ready_ref[kernel, :size, lanes_of(tile)] = piece
            ready_ref[kernel, size:, lanes_of(tile)] = piece

    sums = [sums_ref[probe, k] for k in range(shares)]
    wide = 2 * LANES
    for chunk in range(cols // wide):
        span = slice(chunk * wide, (chunk + 1) * wide)
        up = jnp.where(swapped, near_own_ref[:, :, span], far_own_ref[:, :, span])
        down = jnp.where(swapped, far_own_ref[:, :, span], near_own_ref[:, :, span])
        total = edge_ref[0, :, :, :, span]
        local = jnp.concatenate([up[:, None], down[:, None]], axis=1).astype(F32)
        for kernel in range(kernels):
            term = jnp.dot(fringe_ref[kernel], ready_ref[kernel, :, span], preferred_element_type=F32)
            sums[kernel] = sums[kernel] + fold(term * local.reshape(size, wide))
            total = total + term.reshape(total.shape)
        total_ref[probe, :, :, :, span] = (total * shore_ref[:, :, span].astype(F32)[None]).astype(BF16)

    def copies(p):
        for at, first in ((0, 0), (1, rows - half)):
            yield pltpu.make_async_copy(
                total_ref.at[p, :, at], out_ref.at[p, :, pl.ds(first, half), :], sem.at[p, at]
            )

    for copy in copies(probe):
        copy.start()

    lane = lax.broadcasted_iota(jnp.int32, quad_ref.shape, 1)
    line = jnp.where(probe == 0, 0.0, quad_ref[...])
    for k in range(shares):
        line = jnp.where(lane == probe * shares + k, jnp.sum(sums[k]), line)
    quad_ref[...] = line

    @pl.when(probe == count - 1)
    def _():
        for p in range(count):
            for copy in copies(p):
                copy.wait()


def border(across, fringe, shore, near, far, near_own, far_own, edge, sums, base, half, devices):
    count, variables, rows, cols = base.shape
    kernels = fringe.shape[0]
    size = 2 * half * variables
    planes = pl.BlockSpec((variables, half, cols), lambda p: (p, 0, 0))
    last = pl.BlockSpec((1, half, cols), lambda p: (count * variables, 0, 0))
    keep = pl.BlockSpec(memory_space=pl.ANY)
    return pl.pallas_call(
        functools.partial(border_kernel, half),
        grid=(count,),
        out_shape=(jax.ShapeDtypeStruct(base.shape, BF16), jax.ShapeDtypeStruct((devices, LANES), F32)),
        in_specs=[
            whole(across),
            whole(fringe),
            whole(shore),
            planes,
            planes,
            last,
            last,
            planes,
            planes,
            pl.BlockSpec((1, variables, 2, half, cols), lambda p: (p, 0, 0, 0, 0)),
            whole(sums),
            keep,
        ],
        out_specs=(keep, pl.BlockSpec((devices, LANES), lambda p: (0, 0))),
        scratch_shapes=[
            pltpu.VMEM((size, cols + LANES), BF16),
            pltpu.VMEM((kernels, 2 * size, cols), BF16),
            pltpu.VMEM((count, variables, 2, half, cols), BF16),
            pltpu.SemaphoreType.DMA((count, 2)),
        ],
        input_output_aliases={11: 0},
        compiler_params=pltpu.CompilerParams(vmem_limit_bytes=32 << 20),
        name="border",
    )(across, fringe, shore, near, far, near, far, near_own, far_own, edge, sums, base)


def per_device(probes, filter_taps, mixing, nugget, land_span):
    count, variables, rows, cols = probes.shape
    kernels = filter_taps.shape[0]
    half = filter_taps.shape[2] - 1
    regions, bands = lax.axis_size("region"), lax.axis_size("band")
    inner_pairs = [(i, i ^ 1) for i in range(regions)]
    outer_pairs = [(i, (i + 1 if i % 2 else i - 1) % regions) for i in range(regions)]
    near_pairs = [(i, i ^ 1) for i in range(bands)]
    far_pairs = [(i, i + 1 if i % 2 else i - 1) for i in range(1, bands - 1)]

    probes = pltpu.with_memory_space_constraint(probes, pltpu.HBM)
    span = land_span.reshape(2, 1, rows)
    inner, outer = pack(probes, span, half)
    inner = lax.ppermute(inner, "region", inner_pairs)
    outer = lax.ppermute(outer, "region", outer_pairs)
    near, far, shore, across, downward, fringe = prepare(probes, filter_taps, mixing, span, half)
    near, far = corner(inner, outer, near, far)
    near_halo = lax.ppermute(near, "band", near_pairs)
    far_halo = lax.ppermute(far, "band", far_pairs)
    base, edge, sums = own(mixing, nugget, span, across, downward, probes, inner, outer, half)
    output, quads = border(
        across, fringe, shore, near_halo, far_halo, near, far, edge, sums, base, half, regions * bands
    )
    shares = lax.all_to_all(quads, ("region", "band"), 0, 0, tiled=True)
    quadratic = jnp.sum(shares, axis=0)[: count * (kernels + 1)].reshape(count, kernels + 1)
    return output, quadratic / (bands * rows * cols)


def solution(mesh):
    in_specs = (P(None, None, "band", "region"), P(), P(), P(), P(None, "band", "region"))
    out_specs = (P(None, None, "band", "region"), P())
    return jax.shard_map(
        per_device, mesh=mesh, in_specs=in_specs, out_specs=out_specs, check_vma=False
    )
```

```python
import functools

import jax
import jax.numpy as jnp
from jax import lax
from jax.experimental import pallas as pl
from jax.experimental.pallas import tpu as pltpu
from jax.sharding import PartitionSpec as P

LANES = 128
BF16 = jnp.bfloat16
F32 = jnp.float32
PARTS = 1
SMEM = pl.BlockSpec(memory_space=pltpu.SMEM)


def lanes_of(tile):
    return slice(tile * LANES, (tile + 1) * LANES)


def whole(a):
    return pl.BlockSpec(a.shape, lambda *_: (0,) * len(a.shape))


def odd(axis):
    return lax.axis_index(axis) % 2 != 0


def bounds_by_row(span_ref):
    return [jnp.broadcast_to(span_ref[entry].astype(F32), (LANES, LANES)).T for entry in range(2)]


def land_tile(low, high, first_col):
    column = (lax.broadcasted_iota(jnp.int32, low.shape, 1) + first_col).astype(F32)
    return ((column >= low) & (column < high)).astype(F32).astype(BF16)


def pack_kernel(half, cols, span_ref, west_ref, east_ref, inner_ref, outer_ref):
    probes, variables, _, _ = west_ref.shape
    per_group = LANES // half
    low, high = bounds_by_row(span_ref)
    first = land_tile(low, high, 0)
    last = land_tile(low, high, cols - LANES)
    swapped = odd("region")
    for group in range(inner_ref.shape[0]):
        heads, tails = [], []
        for plane in range(group * per_group, (group + 1) * per_group):
            at = (plane // variables, plane % variables)
            heads.append((west_ref[at] * first)[:, :half])
            tails.append((east_ref[at] * last)[:, LANES - half :])
        left, right = jnp.concatenate(heads, axis=1), jnp.concatenate(tails, axis=1)
        inner_ref[group] = jnp.where(swapped, left, right)
        outer_ref[group] = jnp.where(swapped, right, left)


def pack(probes, span, half):
    count, variables, rows, cols = probes.shape
    edge = jax.ShapeDtypeStruct((count * variables * half // LANES, rows, LANES), BF16)
    tile = lambda at: pl.BlockSpec((count, variables, rows, LANES), lambda _: (0, 0, 0, at))
    kernel = functools.partial(pack_kernel, half, cols)
    return pl.pallas_call(
        kernel,
        grid=(1,),
        out_shape=(edge, edge),
        in_specs=[whole(span), tile(0), tile(cols // LANES - 1)],
        out_specs=(whole(edge), whole(edge)),
        compiler_params=pltpu.CompilerParams(vmem_limit_bytes=16 << 20),
        name="pack",
    )(span, probes, probes)


def prepare_kernel(
    half,
    taps_ref,
    mixing_ref,
    span_ref,
    top_ref,
    bottom_ref,
    near_ref,
    far_ref,
    shore_ref,
    across_ref,
    downward_ref,
    fringe_ref,
):
    probes, variables, _, cols = top_ref.shape
    kernels = downward_ref.shape[0]
    swapped = odd("band")
    low, high = bounds_by_row(span_ref)
    for tile in range(cols // LANES):
        lanes = lanes_of(tile)
        above = land_tile(low[:half], high[:half], tile * LANES)
        below = land_tile(low[-half:], high[-half:], tile * LANES)
        shore_ref[0, :, lanes] = above
        shore_ref[1, :, lanes] = below
        for plane in range(probes * variables):
            at = (plane // variables, plane % variables, slice(None), lanes)
            up, down = top_ref[at] * above, bottom_ref[at] * below
            near_ref[plane, :, lanes] = jnp.where(swapped, up, down)
            far_ref[plane, :, lanes] = jnp.where(swapped, down, up)

    def filtered(kernel, which, distance):
        table = jnp.zeros(distance.shape, F32)
        for tap in range(half + 1):
            table = jnp.where(distance == tap, taps_ref[kernel, which, tap], table)
        return table.astype(BF16)

    def places(shape):
        return lax.broadcasted_iota(jnp.int32, shape, 0), lax.broadcasted_iota(jnp.int32, shape, 1)

    def halves(ref, kernel, first, weight):
        height, width = weight.shape
        parts = ref.shape[2] // width
        for part in range(parts):
            piece = weight.astype(BF16)
            ref[kernel, first : first + height, part * width : (part + 1) * width] = piece
            weight = weight - piece.astype(F32)

    def mixed(kernel, local, v, column, size):
        factor = jnp.zeros(local.shape, F32)
        for w in range(variables):
            factor = jnp.where((column >= w * size) & (column < (w + 1) * size), mixing_ref[kernel, v, w], factor)
        return local * factor

    for kernel in range(kernels):
        row, column = places((across_ref.shape[0], LANES))
        across_ref[:, lanes_of(kernel)] = filtered(kernel, 0, jnp.abs(row - column - half))
        step = downward_ref.shape[1] // variables
        tall = step + 2 * half
        row, column = places((step, variables * tall))
        local = filtered(kernel, 1, jnp.abs((column & (tall - 1)) - half - row)).astype(F32)
        for v in range(variables):
            halves(downward_ref, kernel, v * step, mixed(kernel, local, v, column, tall))
        size = 2 * half
        row, column = places((size, variables * size))
        bits = half.bit_length() - 1
        i, h = row & (half - 1), column & (half - 1)
        upper = (row >> bits) & 1
        gap = jnp.where(upper == 0, i - h, h - i)
        reach = (gap <= 0) & (upper == ((column >> bits) & 1))
        local = filtered(kernel, 1, jnp.where(reach, gap + half, -1)).astype(F32)
        for v in range(variables):
            halves(fringe_ref, kernel, v * size, mixed(kernel, local, v, column, size))


def prepare(probes, taps, mixing, span, half):
    count, variables, rows, cols = probes.shape
    kernels = taps.shape[0]
    size = 2 * half * variables
    strip = jax.ShapeDtypeStruct((count * variables + 1, half, cols), BF16)
    outs = (
        strip,
        strip,
        jax.ShapeDtypeStruct((2, half, cols), BF16),
        jax.ShapeDtypeStruct((2 * LANES, kernels * LANES), BF16),
        jax.ShapeDtypeStruct((kernels, 2 * LANES - 2 * half * variables, PARTS * 2 * LANES), BF16),
        jax.ShapeDtypeStruct((kernels, size, 2 * size), BF16),
    )
    edge = lambda at: pl.BlockSpec((count, variables, half, cols), lambda _: (0, 0, at, 0))
    return pl.pallas_call(
        functools.partial(prepare_kernel, half),
        grid=(1,),
        out_shape=outs,
        in_specs=[SMEM, SMEM, whole(span), edge(0), edge(rows // half - 1)],
        out_specs=tuple(whole(o) for o in outs),
        cost_estimate=pl.CostEstimate(flops=10**7, bytes_accessed=4 << 20, transcendentals=0),
        compiler_params=pltpu.CompilerParams(vmem_limit_bytes=16 << 20),
        name="prepare",
    )(taps, mixing, span, probes, probes)


def corner_kernel(inner_ref, outer_ref, near_in, far_in, near_ref, far_ref):
    half = near_ref.shape[1]
    groups, rows, _ = inner_ref.shape
    swapped = odd("band")
    for at, ref in ((0, inner_ref), (groups, outer_ref)):
        for group in range(groups):
            up, down = ref[group, :half], ref[group, rows - half :]
            near_ref[0, :, lanes_of(at + group)] = jnp.where(swapped, up, down)
            far_ref[0, :, lanes_of(at + group)] = jnp.where(swapped, down, up)
    rest = slice(2 * groups * LANES, near_ref.shape[2])
    near_ref[0, :, rest] = jnp.zeros_like(near_ref[0, :, rest])
    far_ref[0, :, rest] = jnp.zeros_like(far_ref[0, :, rest])


def corner(inner, outer, near, far):
    last = pl.BlockSpec((1, *near.shape[1:]), lambda _: (near.shape[0] - 1, 0, 0))
    keep = pl.BlockSpec(memory_space=pl.ANY)
    return pl.pallas_call(
        corner_kernel,
        grid=(1,),
        out_shape=(jax.ShapeDtypeStruct(near.shape, BF16),) * 2,
        in_specs=[whole(inner), whole(outer), keep, keep],
        out_specs=(last, last),
        input_output_aliases={2: 0, 3: 1},
        compiler_params=pltpu.CompilerParams(vmem_limit_bytes=16 << 20),
        name="corner",
    )(inner, outer, near, far)


def side(block, probe, half, variables):
    per_group = LANES // half // variables
    return pltpu.roll(block.astype(F32), (per_group - probe % per_group) * (half * variables) % LANES, 1)


class Moved:
    def __init__(self, half, height, west, east, tile_of):
        self.half, self.west, self.east, self.tile_of = half, west, east, tile_of
        self.lane = lax.broadcasted_iota(jnp.int32, (height, LANES), 1)
        self.turned = {}

    def turn(self, v, tile):
        if (v, tile) not in self.turned:
            self.turned[v, tile] = pltpu.roll(self.tile_of(v, tile).astype(F32), self.half, 1)
        return self.turned[v, tile]

    def __call__(self, v, tile, tiles):
        half, back = self.half, LANES - self.half * v
        before = self.turn(v, tile - 1) if tile > 0 else pltpu.roll(self.west, back % LANES, 1)
        if tile < tiles:
            after = self.turn(v, tile)
        else:
            after = jnp.where(self.lane < 2 * half, pltpu.roll(self.east, (back + half) % LANES, 1), 0.0)
        return jnp.where(self.lane < half, before, after).astype(BF16)


def fold(part):
    height, width = part.shape
    folded = jnp.sum(part.reshape(height // 8, 8, width), axis=0)
    return sum(folded[:, lanes_of(t)] for t in range(width // LANES))


def own_kernel(
    half,
    nugget_ref,
    span_ref,
    across_ref,
    downward_ref,
    x_ref,
    inner_ref,
    outer_ref,
    out_ref,
    edge_ref,
    sums_ref,
    land_ref,
    ext_ref,
    interior_ref,
):
    probe = pl.program_id(0)
    variables, rows, cols = x_ref.shape[1:]
    kernels = downward_ref.shape[0]
    tiles = cols // LANES

    @pl.when(probe == 0)
    def _():
        low, high = bounds_by_row(span_ref)
        for tile in range(tiles):
            land_ref[:, lanes_of(tile)] = land_tile(low, high, tile * LANES)
        for first in (0, half + rows):
            blank = (slice(None), slice(None), slice(first, first + half), slice(None))
            interior_ref[blank] = jnp.zeros_like(interior_ref[blank])

    group = probe // (LANES // half // variables)
    swapped = odd("region")
    inner, outer = inner_ref[group], outer_ref[group]

    west = side(jnp.where(swapped, inner, outer), probe, half, variables)
    east = side(jnp.where(swapped, outer, inner), probe, half, variables)
    moved = Moved(half, rows, west, east, lambda v, t: x_ref[0, v, :, lanes_of(t)] * land_ref[:, lanes_of(t)])
    sums = [jnp.zeros((8, LANES), F32) for _ in range(kernels + 1)]
    wide = 2 * LANES
    step = downward_ref.shape[1] // variables
    parts = downward_ref.shape[2] // wide

    def filter_columns(chunk):
        first, past = 2 * chunk, 2 * chunk + 2
        for v in range(variables):
            for tile in range(first + (chunk > 0), past + 1):
                ext_ref[v, :, lanes_of(tile)] = moved(v, tile, tiles)
        for tile in range(first, past):
            window = ext_ref[:, :, tile * LANES : (tile + 2) * LANES].reshape(variables * rows, wide)
            both = jnp.dot(window, across_ref[...], preferred_element_type=F32).astype(BF16)
            for kernel in range(kernels):
                interior_ref[kernel, :, half : half + rows, lanes_of(tile)] = both[:, lanes_of(kernel)].reshape(
                    variables, rows, LANES
                )

    def filter_rows(chunk):
        span = slice(chunk * wide, (chunk + 1) * wide)
        for first in range(0, rows, step):
            here = slice(first, first + step)
            terms = []
            for kernel in range(kernels):
                window = interior_ref[kernel, :, first : first + step + 2 * half, span].reshape(wide, wide)
                window = jnp.concatenate([window] * parts, axis=0)
                terms.append(jnp.dot(downward_ref[kernel], window, preferred_element_type=F32))
            land = land_ref[here, span]
            for v in range(variables):
                local = (x_ref[0, v, here, span] * land).astype(F32)
                total = nugget_ref[v] * local
                sums[kernels] = sums[kernels] + fold(total * local)
                for kernel in range(kernels):
                    term = terms[kernel][v * step : (v + 1) * step]
                    sums[kernel] = sums[kernel] + fold(term * local)
                    total = total + term
                out_ref[0, v, here, span] = total.astype(BF16) * land
                if first == 0:
                    edge_ref[0, v, 0, :, span] = total[:half]
                if first + step == rows:
                    edge_ref[0, v, 1, :, span] = total[step - half :]

    filter_columns(0)
    for chunk in range(cols // wide):
        if chunk + 1 < cols // wide:
            filter_columns(chunk + 1)
        filter_rows(chunk)
    for k in range(kernels + 1):
        sums_ref[0, k] = sums[k]


def own(nugget, span, across, downward, probes, inner, outer, half):
    count, variables, rows, cols = probes.shape
    kernels = downward.shape[0]
    block = lambda *shape: pl.BlockSpec((1, *shape), lambda p: (p,) + (0,) * len(shape))
    outs = (
        jax.ShapeDtypeStruct(probes.shape, BF16),
        jax.ShapeDtypeStruct((count, variables, 2, half, cols), F32),
        jax.ShapeDtypeStruct((count, kernels + 1, 8, LANES), F32),
    )
    return pl.pallas_call(
        functools.partial(own_kernel, half),
        grid=(count,),
        out_shape=outs,
        in_specs=[
            SMEM,
            whole(span),
            whole(across),
            whole(downward),
            block(*probes.shape[1:]),
            whole(inner),
            whole(outer),
        ],
        out_specs=tuple(block(*o.shape[1:]) for o in outs),
        scratch_shapes=[
            pltpu.VMEM((rows, cols), BF16),
            pltpu.VMEM((variables, rows, cols + LANES), BF16),
            pltpu.VMEM((kernels, variables, rows + 2 * half, cols), BF16),
        ],
        cost_estimate=pl.CostEstimate(flops=10**10, bytes_accessed=16 << 20, transcendentals=0),
        compiler_params=pltpu.CompilerParams(vmem_limit_bytes=32 << 20),
        name="own",
    )(nugget, span, across, downward, probes, inner, outer)


def border_kernel(
    half,
    across_ref,
    fringe_ref,
    shore_ref,
    near_ref,
    far_ref,
    near_own_ref,
    far_own_ref,
    edge_ref,
    sums_ref,
    base_ref,
    out_ref,
    quad_ref,
    ext_ref,
    ready_ref,
    total_ref,
    sem,
):
    count, variables, _, _, cols = edge_ref.shape
    rows = out_ref.shape[2]
    shares = sums_ref.shape[1]
    kernels = shares - 1
    tiles = cols // LANES
    per_group = LANES // half // variables
    groups = count // per_group
    swapped, flipped = odd("band"), odd("region")
    size = 2 * half * variables
    wide = 2 * LANES
    last = count * variables

    for at in range(2):
        from_near = swapped if at == 0 else jnp.logical_not(swapped)

        def halo(plane, lanes, from_near=from_near):
            return jnp.where(from_near, near_ref[plane, :, lanes], far_ref[plane, :, lanes])

        for p in range(count):
            inner, outer = (halo(last, lanes_of(kind + p // per_group)) for kind in (0, groups))
            west = side(jnp.where(flipped, inner, outer), p, half, variables)
            east = side(jnp.where(flipped, outer, inner), p, half, variables)
            moved = Moved(half, half, west, east, lambda v, t, p=p: halo(p * variables + v, lanes_of(t)))
            for v in range(variables):
                first = (2 * v + at) * half
                for tile in range(tiles + 1):
                    ext_ref[p, first : first + half, lanes_of(tile)] = moved(v, tile, tiles)

    def filter_columns(tile):
        window = ext_ref[:, :, tile * LANES : (tile + 2) * LANES].reshape(count * size, wide)
        both = jnp.dot(window, across_ref[...], preferred_element_type=F32).astype(BF16)
        for kernel in range(kernels):
            piece = both[:, lanes_of(kernel)].reshape(count, size, LANES)
            ready_ref[kernel, :, :size, lanes_of(tile)] = piece
            ready_ref[kernel, :, size:, lanes_of(tile)] = piece

    sums = {(p, k): sums_ref[p, k] for p in range(count) for k in range(shares)}

    def filter_rows(chunk):
        span = slice(chunk * wide, (chunk + 1) * wide)
        shore = shore_ref[:, :, span]
        for p in range(count):
            planes = slice(p * variables, (p + 1) * variables)
            near, far = near_own_ref[planes, :, span], far_own_ref[planes, :, span]
            up, down = jnp.where(swapped, near, far), jnp.where(swapped, far, near)
            total = edge_ref[p, :, :, :, span]
            local = jnp.concatenate([up[:, None], down[:, None]], axis=1).astype(F32)
            for kernel in range(kernels):
                term = jnp.dot(fringe_ref[kernel], ready_ref[kernel, p, :, span], preferred_element_type=F32)
                sums[p, kernel] = sums[p, kernel] + fold(term * local.reshape(size, wide))
                total = total + term.reshape(total.shape)
            total_ref[p, :, :, :, span] = total.astype(BF16) * shore[None]

    chunks = cols // wide
    for tile in (0, 1):
        filter_columns(tile)
    for chunk in range(chunks):
        for tile in (2 * chunk + 2, 2 * chunk + 3):
            if tile < tiles:
                filter_columns(tile)
        filter_rows(chunk)

    copies = [
        pltpu.make_async_copy(total_ref.at[:, :, at], out_ref.at[:, :, pl.ds(first, half), :], sem.at[at])
        for at, first in ((0, 0), (1, rows - half))
    ]
    for copy in copies:
        copy.start()

    lane = lax.broadcasted_iota(jnp.int32, quad_ref.shape, 1)
    line = jnp.zeros(quad_ref.shape, F32)
    for (p, k), part in sums.items():
        line = jnp.where(lane == p * shares + k, jnp.sum(part), line)
    quad_ref[...] = line
    for copy in copies:
        copy.wait()


def border(across, fringe, shore, near, far, near_own, far_own, edge, sums, base, half, devices):
    count, variables, rows, cols = base.shape
    kernels = fringe.shape[0]
    size = 2 * half * variables
    keep = pl.BlockSpec(memory_space=pl.ANY)
    quads = jax.ShapeDtypeStruct((devices, LANES), F32)
    operands = (across, fringe, shore, near, far, near_own, far_own, edge, sums)
    return pl.pallas_call(
        functools.partial(border_kernel, half),
        grid=(1,),
        out_shape=(jax.ShapeDtypeStruct(base.shape, BF16), quads),
        in_specs=[whole(o) for o in operands] + [keep],
        out_specs=(keep, whole(quads)),
        scratch_shapes=[
            pltpu.VMEM((count, size, cols + LANES), BF16),
            pltpu.VMEM((kernels, count, 2 * size, cols), BF16),
            pltpu.VMEM((count, variables, 2, half, cols), BF16),
            pltpu.SemaphoreType.DMA((2,)),
        ],
        input_output_aliases={len(operands): 0},
        compiler_params=pltpu.CompilerParams(vmem_limit_bytes=32 << 20),
        name="border",
    )(*operands, base)


def per_device(probes, filter_taps, mixing, nugget, land_span):
    count, variables, rows, cols = probes.shape
    kernels = filter_taps.shape[0]
    half = filter_taps.shape[2] - 1
    regions, bands = lax.axis_size("region"), lax.axis_size("band")
    inner_pairs = [(i, i ^ 1) for i in range(regions)]
    outer_pairs = [(i, (i + 1 if i % 2 else i - 1) % regions) for i in range(regions)]
    near_pairs = [(i, i ^ 1) for i in range(bands)]
    far_pairs = [(i, i + 1 if i % 2 else i - 1) for i in range(1, bands - 1)]

    probes = pltpu.with_memory_space_constraint(probes, pltpu.HBM)
    span = pltpu.with_memory_space_constraint(land_span.reshape(2, 1, rows), pltpu.HBM)
    inner, outer = pack(probes, span, half)
    inner = lax.ppermute(inner, "region", inner_pairs)
    outer = lax.ppermute(outer, "region", outer_pairs)
    near, far, shore, across, downward, fringe = prepare(probes, filter_taps, mixing, span, half)
    near, far = corner(inner, outer, near, far)
    near_halo = lax.ppermute(near, "band", near_pairs)
    far_halo = lax.ppermute(far, "band", far_pairs)
    base, edge, sums = own(nugget, span, across, downward, probes, inner, outer, half)
    output, quads = border(
        across, fringe, shore, near_halo, far_halo, near, far, edge, sums, base, half, regions * bands
    )
    shares = lax.all_to_all(quads, ("region", "band"), 0, 0, tiled=True)
    quadratic = jnp.sum(shares, axis=0)[: count * (kernels + 1)].reshape(count, kernels + 1)
    return output, quadratic / (bands * rows * cols)


def solution(mesh):
    in_specs = (P(None, None, "band", "region"), P(), P(), P(), P(None, "band", "region"))
    out_specs = (P(None, None, "band", "region"), P())
    return jax.shard_map(
        per_device, mesh=mesh, in_specs=in_specs, out_specs=out_specs, check_vma=False
    )
```

```python
import functools

import jax
import jax.numpy as jnp
from jax import lax
from jax.experimental import pallas as pl
from jax.experimental.pallas import tpu as pltpu
from jax.sharding import PartitionSpec as P

LANES = 128
BF16 = jnp.bfloat16
F32 = jnp.float32
PARTS = 1
SMEM = pl.BlockSpec(memory_space=pltpu.SMEM)


def lanes_of(tile):
    return slice(tile * LANES, (tile + 1) * LANES)


def whole(a):
    return pl.BlockSpec(a.shape, lambda *_: (0,) * len(a.shape))


def odd(axis):
    return lax.axis_index(axis) % 2 != 0


def bounds_by_row(span_ref):
    return [jnp.broadcast_to(span_ref[entry].astype(F32), (LANES, LANES)).T for entry in range(2)]


def land_tile(low, high, first_col):
    column = (lax.broadcasted_iota(jnp.int32, low.shape, 1) + first_col).astype(F32)
    return ((column >= low) & (column < high)).astype(F32).astype(BF16)


def pack_kernel(half, cols, outer, span_ref, x_ref, edge_ref, tile_ref, sem):
    _, variables, _, _ = x_ref.shape
    per_group = LANES // half
    east = odd("region") == outer
    first = pl.multiple_of(jnp.where(east, cols - LANES, 0), LANES)
    copy = pltpu.make_async_copy(x_ref.at[:, :, :, pl.ds(first, LANES)], tile_ref, sem)
    copy.start()
    low, high = bounds_by_row(span_ref)
    land = land_tile(low, high, first)
    copy.wait()
    for group in range(edge_ref.shape[0]):
        pieces = []
        for plane in range(group * per_group, (group + 1) * per_group):
            tile = tile_ref[plane // variables, plane % variables] * land
            pieces.append(jnp.where(east, tile[:, LANES - half :], tile[:, :half]))
        edge_ref[group] = jnp.concatenate(pieces, axis=1)


def pack(probes, span, half, outer):
    count, variables, rows, cols = probes.shape
    edge = jax.ShapeDtypeStruct((count * variables * half // LANES, rows, LANES), BF16)
    return pl.pallas_call(
        functools.partial(pack_kernel, half, cols, outer),
        grid=(1,),
        out_shape=edge,
        in_specs=[whole(span), pl.BlockSpec(memory_space=pl.ANY)],
        out_specs=whole(edge),
        scratch_shapes=[pltpu.VMEM((count, variables, rows, LANES), BF16), pltpu.SemaphoreType.DMA],
        cost_estimate=pl.CostEstimate(flops=10**6, bytes_accessed=1 << 20, transcendentals=0),
        compiler_params=pltpu.CompilerParams(vmem_limit_bytes=16 << 20),
        name="pack",
    )(span, probes)


def prepare_kernel(
    half,
    taps_ref,
    mixing_ref,
    span_ref,
    x_ref,
    masked_ref,
    near_ref,
    far_ref,
    land_ref,
    across_ref,
    downward_ref,
    fringe_ref,
):
    probe = pl.program_id(0)
    variables, rows, cols = x_ref.shape[1:]
    tiles = cols // LANES
    swapped = odd("band")

    @pl.when(probe == 0)
    def _():
        low, high = bounds_by_row(span_ref)
        for tile in range(tiles):
            land_ref[tile] = land_tile(low, high, tile * LANES)

    for tile in range(tiles):
        land = land_ref[tile]
        for v in range(variables):
            plane = probe * variables + v
            value = x_ref[0, v, :, lanes_of(tile)] * land
            masked_ref[plane, tile] = value
            up, down = value[:half], value[rows - half :]
            near_ref[plane, tile] = jnp.where(swapped, up, down)
            far_ref[plane, tile] = jnp.where(swapped, down, up)

    @pl.when(probe == pl.num_programs(0) - 1)
    def _():
        make_tables(half, variables, taps_ref, mixing_ref, across_ref, downward_ref, fringe_ref)


def make_tables(half, variables, taps_ref, mixing_ref, across_ref, downward_ref, fringe_ref):
    kernels = downward_ref.shape[0]
    swapped = odd("band")

    def filtered(kernel, which, distance):
        table = jnp.zeros(distance.shape, F32)
        for tap in range(half + 1):
            table = jnp.where(distance == tap, taps_ref[kernel, which, tap], table)
        return table.astype(BF16)

    def places(shape):
        return lax.broadcasted_iota(jnp.int32, shape, 0), lax.broadcasted_iota(jnp.int32, shape, 1)

    def halves(ref, kernel, first, weight):
        height, width = weight.shape
        parts = ref.shape[2] // width
        for part in range(parts):
            piece = weight.astype(BF16)
            ref[kernel, first : first + height, part * width : (part + 1) * width] = piece
            weight = weight - piece.astype(F32)

    def mixed(kernel, local, v, column, size):
        factor = jnp.zeros(local.shape, F32)
        for w in range(variables):
            factor = jnp.where((column >= w * size) & (column < (w + 1) * size), mixing_ref[kernel, v, w], factor)
        return local * factor

    for kernel in range(kernels):
        row, column = places((LANES, LANES))
        across_ref[:LANES, lanes_of(kernel)] = filtered(kernel, 0, jnp.abs(row - column))
        gap = jnp.where(row < LANES // 2, LANES + row - column, LANES - row + column)
        across_ref[LANES:, lanes_of(kernel)] = filtered(kernel, 0, gap)
        step = downward_ref.shape[1] // variables
        tall = step + 2 * half
        row, column = places((step, variables * tall))
        local = filtered(kernel, 1, jnp.abs((column & (tall - 1)) - half - row)).astype(F32)
        for v in range(variables):
            halves(downward_ref, kernel, v * step, mixed(kernel, local, v, column, tall))
        size = 2 * half
        row, column = places((size, variables * size))
        bits = half.bit_length() - 1
        i, h = row & (half - 1), column & (half - 1)
        which = (row >> bits) & 1
        gap = jnp.where((which == 0) == swapped, i - h, h - i)
        reach = (gap <= 0) & (which == ((column >> bits) & 1))
        local = filtered(kernel, 1, jnp.where(reach, gap + half, -1)).astype(F32)
        for v in range(variables):
            halves(fringe_ref, kernel, v * size, mixed(kernel, local, v, column, size))


def prepare(probes, taps, mixing, span, half):
    count, variables, rows, cols = probes.shape
    kernels = taps.shape[0]
    planes, tiles = count * variables, cols // LANES
    size = 2 * half * variables
    strip = jax.ShapeDtypeStruct((planes + 1, tiles, half, LANES), BF16)
    outs = (
        jax.ShapeDtypeStruct((planes, tiles, rows, LANES), BF16),
        strip,
        strip,
        jax.ShapeDtypeStruct((tiles, rows, LANES), BF16),
        jax.ShapeDtypeStruct((2 * LANES, kernels * LANES), BF16),
        jax.ShapeDtypeStruct((kernels, 2 * LANES - 2 * half * variables, PARTS * 2 * LANES), BF16),
        jax.ShapeDtypeStruct((kernels, size, PARTS * size), BF16),
    )
    return pl.pallas_call(
        functools.partial(prepare_kernel, half),
        grid=(count,),
        out_shape=outs,
        in_specs=[SMEM, SMEM, whole(span), pl.BlockSpec((1, *probes.shape[1:]), lambda p: (p, 0, 0, 0))],
        out_specs=tuple(whole(o) for o in outs),
        cost_estimate=pl.CostEstimate(flops=10**7, bytes_accessed=4 << 20, transcendentals=0),
        compiler_params=pltpu.CompilerParams(vmem_limit_bytes=16 << 20),
        name="prepare",
    )(taps, mixing, span, probes)


def corner_kernel(inner_ref, outer_ref, near_in, far_in, near_ref, far_ref):
    tiles, half = near_ref.shape[1:3]
    groups, rows, _ = inner_ref.shape
    swapped = odd("band")
    for at, ref in ((0, inner_ref), (groups, outer_ref)):
        for group in range(groups):
            up, down = ref[group, :half], ref[group, rows - half :]
            near_ref[0, at + group] = jnp.where(swapped, up, down)
            far_ref[0, at + group] = jnp.where(swapped, down, up)
    for tile in range(2 * groups, tiles):
        near_ref[0, tile] = jnp.zeros_like(near_ref[0, tile])
        far_ref[0, tile] = jnp.zeros_like(far_ref[0, tile])


def corner(inner, outer, near, far):
    last = pl.BlockSpec((1, *near.shape[1:]), lambda _: (near.shape[0] - 1, 0, 0, 0))
    keep = pl.BlockSpec(memory_space=pl.ANY)
    return pl.pallas_call(
        corner_kernel,
        grid=(1,),
        out_shape=(jax.ShapeDtypeStruct(near.shape, BF16),) * 2,
        in_specs=[whole(inner), whole(outer), keep, keep],
        out_specs=(last, last),
        input_output_aliases={2: 0, 3: 1},
        compiler_params=pltpu.CompilerParams(vmem_limit_bytes=16 << 20),
        name="corner",
    )(inner, outer, near, far)


def around(tile_of, v, tile, tiles, west, east, probe, half, variables):
    slot = (probe % (LANES // half // variables)) * variables + v

    def line_up(block, lane):
        return pltpu.roll(block.astype(F32), (lane + LANES - half * slot) % LANES, 1).astype(BF16)

    before = tile_of(v, tile - 1) if tile > 0 else line_up(west, LANES - half)
    after = tile_of(v, tile + 1) if tile + 1 < tiles else line_up(east, 0)
    lane = lax.broadcasted_iota(jnp.int32, before.shape, 1)
    return jnp.where(lane < LANES // 2, after, before)


def fold(part):
    height, width = part.shape
    folded = jnp.sum(part.reshape(height // 8, 8, width), axis=0)
    return sum(folded[:, lanes_of(t)] for t in range(width // LANES))


def own_kernel(
    half,
    nugget_ref,
    across_ref,
    downward_ref,
    masked_ref,
    land_ref,
    inner_ref,
    outer_ref,
    out_ref,
    edge_ref,
    sums_ref,
    interior_ref,
):
    probe = pl.program_id(0)
    variables, rows, cols = out_ref.shape[1:]
    kernels = downward_ref.shape[0]
    tiles = cols // LANES
    upper = jnp.where(odd("band"), 0, 1)

    @pl.when(probe == 0)
    def _():
        for first in (0, half + rows):
            blank = (slice(None),) * 3 + (slice(first, first + half), slice(None))
            interior_ref[blank] = jnp.zeros_like(interior_ref[blank])

    group = probe // (LANES // half // variables)
    swapped = odd("region")
    inner, outer = inner_ref[group], outer_ref[group]

    west, east = jnp.where(swapped, inner, outer), jnp.where(swapped, outer, inner)

    def tile_of(v, tile):
        return masked_ref[probe * variables + v, tile]

    sums = [jnp.zeros((8, LANES), F32) for _ in range(kernels + 1)]
    wide = 2 * LANES
    step = downward_ref.shape[1] // variables
    parts = downward_ref.shape[2] // wide

    def filter_columns(chunk):
        for tile in (2 * chunk, 2 * chunk + 1):
            window = []
            for v in range(variables):
                sides = around(tile_of, v, tile, tiles, west, east, probe, half, variables)
                window.append(jnp.concatenate([tile_of(v, tile), sides], axis=1))
            window = jnp.concatenate(window, axis=0)
            both = jnp.dot(window, across_ref[...], preferred_element_type=F32).astype(BF16)
            for kernel in range(kernels):
                interior_ref[kernel, :, tile, half : half + rows] = both[:, lanes_of(kernel)].reshape(
                    variables, rows, LANES
                )

    def filter_rows(chunk):
        span = slice(chunk * wide, (chunk + 1) * wide)
        for first in range(0, rows, step):
            here = slice(first, first + step)
            terms = []
            for kernel in range(kernels):
                window = jnp.concatenate(
                    [
                        interior_ref[kernel, :, tile, first : first + step + 2 * half].reshape(wide, LANES)
                        for tile in (2 * chunk, 2 * chunk + 1)
                    ],
                    axis=1,
                )
                window = jnp.concatenate([window] * parts, axis=0)
                terms.append(jnp.dot(downward_ref[kernel], window, preferred_element_type=F32))
            land = jnp.concatenate([land_ref[2 * chunk, here], land_ref[2 * chunk + 1, here]], axis=1)
            for v in range(variables):
                plane = probe * variables + v
                local = jnp.concatenate(
                    [masked_ref[plane, 2 * chunk, here], masked_ref[plane, 2 * chunk + 1, here]], axis=1
                ).astype(F32)
                total = nugget_ref[v] * local
                sums[kernels] = sums[kernels] + fold(total * local)
                for kernel in range(kernels):
                    term = terms[kernel][v * step : (v + 1) * step]
                    sums[kernel] = sums[kernel] + fold(term * local)
                    total = total + term
                out_ref[0, v, here, span] = total.astype(BF16) * land
                if first == 0:
                    edge_ref[0, v, upper, :, span] = total[:half]
                if first + step == rows:
                    edge_ref[0, v, 1 - upper, :, span] = total[step - half :]

    filter_columns(0)
    for chunk in range(cols // wide):
        if chunk + 1 < cols // wide:
            filter_columns(chunk + 1)
        filter_rows(chunk)
    for k in range(kernels + 1):
        sums_ref[0, k] = sums[k]


def own(nugget, across, downward, masked, land, inner, outer, half, shape):
    count, variables, rows, cols = shape
    kernels = downward.shape[0]
    block = lambda *shape: pl.BlockSpec((1, *shape), lambda p: (p,) + (0,) * len(shape))
    outs = (
        jax.ShapeDtypeStruct(shape, BF16),
        jax.ShapeDtypeStruct((count, variables, 2, half, cols), F32),
        jax.ShapeDtypeStruct((count, kernels + 1, 8, LANES), F32),
    )
    operands = (across, downward, masked, land, inner, outer)
    return pl.pallas_call(
        functools.partial(own_kernel, half),
        grid=(count,),
        out_shape=outs,
        in_specs=[SMEM] + [whole(o) for o in operands],
        out_specs=tuple(block(*o.shape[1:]) for o in outs),
        scratch_shapes=[pltpu.VMEM((kernels, variables, cols // LANES, rows + 2 * half, LANES), BF16)],
        cost_estimate=pl.CostEstimate(flops=10**10, bytes_accessed=16 << 20, transcendentals=0),
        compiler_params=pltpu.CompilerParams(vmem_limit_bytes=32 << 20),
        name="own",
    )(nugget, *operands)


def border_kernel(
    half,
    across_ref,
    fringe_ref,
    land_ref,
    near_ref,
    far_ref,
    near_own_ref,
    far_own_ref,
    edge_ref,
    sums_ref,
    base_ref,
    out_ref,
    quad_ref,
    ready_ref,
    total_ref,
    sem,
):
    count, variables, _, _, cols = edge_ref.shape
    rows = out_ref.shape[2]
    shares = sums_ref.shape[1]
    kernels = shares - 1
    tiles = cols // LANES
    per_group = LANES // half // variables
    groups = count // per_group
    flipped = odd("region")
    upper = jnp.where(odd("band"), 0, rows - half)
    firsts = [pl.multiple_of(upper, half), pl.multiple_of(rows - half - upper, half)]
    size = 2 * half * variables
    wide = 2 * LANES
    last = count * variables

    halos = (near_ref, far_ref)

    def corners(ref, p):
        inner, outer = (ref[last, kind + p // per_group] for kind in (0, groups))
        return jnp.where(flipped, inner, outer), jnp.where(flipped, outer, inner)

    ends = {(at, p): corners(halos[at], p) for at in range(2) for p in range(count)}

    def filter_columns(tile):
        window = []
        for p in range(count):
            for v in range(variables):
                for at in range(2):
                    tile_of = lambda v, t: halos[at][p * variables + v, t]
                    sides = around(tile_of, v, tile, tiles, *ends[at, p], p, half, variables)
                    window.append(jnp.concatenate([tile_of(v, tile), sides], axis=1))
        window = jnp.concatenate(window, axis=0)
        both = jnp.dot(window, across_ref[...], preferred_element_type=F32).astype(BF16)
        for kernel in range(kernels):
            piece = both[:, lanes_of(kernel)].reshape(count, size, LANES)
            ready_ref[kernel, :, tile] = piece

    sums = {(p, k): sums_ref[p, k] for p in range(count) for k in range(shares)}

    def filter_rows(chunk):
        span = slice(chunk * wide, (chunk + 1) * wide)
        pair = (2 * chunk, 2 * chunk + 1)
        strips = [
            jnp.concatenate([land_ref[tile, pl.ds(first, half)] for tile in pair], axis=1) for first in firsts
        ]
        shore = jnp.stack(strips)
        for p in range(count):
            planes = slice(p * variables, (p + 1) * variables)
            near, far = (
                jnp.concatenate([ref[planes, tile] for tile in pair], axis=2) for ref in (near_own_ref, far_own_ref)
            )
            total = edge_ref[p, :, :, :, span]
            local = jnp.stack([near, far], axis=1).astype(F32)
            for kernel in range(kernels):
                window = jnp.concatenate([ready_ref[kernel, p, tile] for tile in pair], axis=1)
                window = jnp.concatenate([window] * (fringe_ref.shape[2] // size), axis=0)
                term = jnp.dot(fringe_ref[kernel], window, preferred_element_type=F32)
                sums[p, kernel] = sums[p, kernel] + fold(term * local.reshape(size, wide))
                total = total + term.reshape(total.shape)
            total_ref[p, :, :, :, span] = total.astype(BF16) * shore[None]

    chunks = cols // wide
    for tile in (0, 1):
        filter_columns(tile)
    for chunk in range(chunks):
        for tile in (2 * chunk + 2, 2 * chunk + 3):
            if tile < tiles:
                filter_columns(tile)
        filter_rows(chunk)

    copies = [
        pltpu.make_async_copy(total_ref.at[:, :, at], out_ref.at[:, :, pl.ds(first, half), :], sem.at[at])
        for at, first in enumerate(firsts)
    ]
    for copy in copies:
        copy.start()

    lane = lax.broadcasted_iota(jnp.int32, quad_ref.shape, 1)
    line = jnp.zeros(quad_ref.shape, F32)
    for (p, k), part in sums.items():
        line = jnp.where(lane == p * shares + k, jnp.sum(part), line)
    quad_ref[...] = line
    for copy in copies:
        copy.wait()


def border(across, fringe, land, near, far, near_own, far_own, edge, sums, base, half, devices):
    count, variables, _, cols = base.shape
    kernels = fringe.shape[0]
    size = 2 * half * variables
    keep = pl.BlockSpec(memory_space=pl.ANY)
    quads = jax.ShapeDtypeStruct((devices, LANES), F32)
    operands = (across, fringe, land, near, far, near_own, far_own, edge, sums)
    return pl.pallas_call(
        functools.partial(border_kernel, half),
        grid=(1,),
        out_shape=(jax.ShapeDtypeStruct(base.shape, BF16), quads),
        in_specs=[whole(o) for o in operands] + [keep],
        out_specs=(keep, whole(quads)),
        scratch_shapes=[
            pltpu.VMEM((kernels, count, cols // LANES, size, LANES), BF16),
            pltpu.VMEM((count, variables, 2, half, cols), BF16),
            pltpu.SemaphoreType.DMA((2,)),
        ],
        input_output_aliases={len(operands): 0},
        compiler_params=pltpu.CompilerParams(vmem_limit_bytes=32 << 20),
        name="border",
    )(*operands, base)


def per_device(probes, filter_taps, mixing, nugget, land_span):
    count, _, rows, cols = probes.shape
    kernels = filter_taps.shape[0]
    half = filter_taps.shape[2] - 1
    regions, bands = lax.axis_size("region"), lax.axis_size("band")
    inner_pairs = [(i, i ^ 1) for i in range(regions)]
    outer_pairs = [(i, (i + 1 if i % 2 else i - 1) % regions) for i in range(regions)]
    near_pairs = [(i, i ^ 1) for i in range(bands)]
    far_pairs = [(i, i + 1 if i % 2 else i - 1) for i in range(1, bands - 1)]

    probes = pltpu.with_memory_space_constraint(probes, pltpu.HBM)
    span = pltpu.with_memory_space_constraint(land_span.reshape(2, 1, rows), pltpu.HBM)
    outer = pack(probes, span, half, True)
    outer = lax.ppermute(outer, "region", outer_pairs)
    inner = pack(probes, span, half, False)
    inner = lax.ppermute(inner, "region", inner_pairs)
    masked, near, far, land, across, downward, fringe = prepare(probes, filter_taps, mixing, span, half)
    near, far = corner(inner, outer, near, far)
    near_halo = lax.ppermute(near, "band", near_pairs)
    far_halo = lax.ppermute(far, "band", far_pairs)
    base, edge, sums = own(nugget, across, downward, masked, land, inner, outer, half, probes.shape)
    output, quads = border(
        across, fringe, land, near_halo, far_halo, near, far, edge, sums, base, half, regions * bands
    )
    shares = lax.all_to_all(quads, ("region", "band"), 0, 0, tiled=True)
    quadratic = jnp.sum(shares, axis=0)[: count * (kernels + 1)].reshape(count, kernels + 1)
    return output, quadratic / (bands * rows * cols)


def solution(mesh):
    in_specs = (P(None, None, "band", "region"), P(), P(), P(), P(None, "band", "region"))
    out_specs = (P(None, None, "band", "region"), P())
    return jax.shard_map(
        per_device, mesh=mesh, in_specs=in_specs, out_specs=out_specs, check_vma=False
    )
```

```python
import functools

import jax
import jax.numpy as jnp
from jax import lax
from jax.experimental import pallas as pl
from jax.experimental.pallas import tpu as pltpu
from jax.sharding import PartitionSpec as P

LANES = 128
BF16 = jnp.bfloat16
F32 = jnp.float32
PARTS = 1
SMEM = pl.BlockSpec(memory_space=pltpu.SMEM)


def lanes_of(tile):
    return slice(tile * LANES, (tile + 1) * LANES)


def whole(a):
    return pl.BlockSpec(a.shape, lambda *_: (0,) * len(a.shape))


def odd(axis):
    return lax.axis_index(axis) % 2 != 0


def bounds_by_row(span_ref):
    return [jnp.broadcast_to(span_ref[entry].astype(F32), (LANES, LANES)).T for entry in range(2)]


def land_tile(low, high, first_col):
    column = (lax.broadcasted_iota(jnp.int32, low.shape, 1) + first_col).astype(F32)
    return ((column >= low) & (column < high)).astype(F32).astype(BF16)


def pack_kernel(half, cols, span_ref, west_ref, east_ref, inner_ref, outer_ref):
    variables = west_ref.shape[1]
    per_group = LANES // half
    low, high = bounds_by_row(span_ref)
    first = land_tile(low, high, 0)
    last = land_tile(low, high, cols - LANES)
    swapped = odd("region")
    for group in range(inner_ref.shape[0]):
        heads, tails = [], []
        for plane in range(group * per_group, (group + 1) * per_group):
            at = (plane // variables, plane % variables)
            heads.append((west_ref[at] * first)[:, :half])
            tails.append((east_ref[at] * last)[:, LANES - half :])
        left, right = jnp.concatenate(heads, axis=1), jnp.concatenate(tails, axis=1)
        inner_ref[group] = jnp.where(swapped, left, right)
        outer_ref[group] = jnp.where(swapped, right, left)


def pack(probes, span, half):
    count, variables, rows, cols = probes.shape
    groups = count * variables * half // LANES
    steps = 1
    edge = jax.ShapeDtypeStruct((groups, rows, LANES), BF16)
    tile = lambda at: pl.BlockSpec((count // steps, variables, rows, LANES), lambda g: (g, 0, 0, at))
    piece = pl.BlockSpec((groups // steps, rows, LANES), lambda g: (g, 0, 0))
    return pl.pallas_call(
        functools.partial(pack_kernel, half, cols),
        grid=(steps,),
        out_shape=(edge, edge),
        in_specs=[whole(span), tile(0), tile(cols // LANES - 1)],
        out_specs=(piece, piece),
        compiler_params=pltpu.CompilerParams(vmem_limit_bytes=16 << 20),
        name="pack",
    )(span, probes, probes)


def prepare_kernel(
    half,
    taps_ref,
    mixing_ref,
    span_ref,
    x_ref,
    masked_ref,
    near_ref,
    far_ref,
    land_ref,
    across_ref,
    downward_ref,
    fringe_ref,
):
    probe = pl.program_id(0)
    variables, rows, cols = x_ref.shape[1:]
    tiles = cols // LANES
    swapped = odd("band")

    @pl.when(probe == 0)
    def _():
        low, high = bounds_by_row(span_ref)
        for tile in range(tiles):
            land_ref[tile] = land_tile(low, high, tile * LANES)

    for tile in range(tiles):
        land = land_ref[tile]
        for v in range(variables):
            plane = probe * variables + v
            value = x_ref[0, v, :, lanes_of(tile)] * land
            masked_ref[plane, tile] = value
            up, down = value[:half], value[rows - half :]
            near_ref[plane, tile] = jnp.where(swapped, up, down)
            far_ref[plane, tile] = jnp.where(swapped, down, up)

    @pl.when(probe == pl.num_programs(0) - 1)
    def _():
        make_tables(half, variables, taps_ref, mixing_ref, across_ref, downward_ref, fringe_ref)


def make_tables(half, variables, taps_ref, mixing_ref, across_ref, downward_ref, fringe_ref):
    kernels = downward_ref.shape[0]
    swapped = odd("band")

    def filtered(kernel, which, distance):
        table = jnp.zeros(distance.shape, F32)
        for tap in range(half + 1):
            table = jnp.where(distance == tap, taps_ref[kernel, which, tap], table)
        return table.astype(BF16)

    def places(shape):
        return lax.broadcasted_iota(jnp.int32, shape, 0), lax.broadcasted_iota(jnp.int32, shape, 1)

    def halves(ref, kernel, first, weight):
        height, width = weight.shape
        parts = ref.shape[2] // width
        for part in range(parts):
            piece = weight.astype(BF16)
            ref[kernel, first : first + height, part * width : (part + 1) * width] = piece
            weight = weight - piece.astype(F32)

    def mixed(kernel, local, v, column, size):
        factor = jnp.zeros(local.shape, F32)
        for w in range(variables):
            factor = jnp.where((column >= w * size) & (column < (w + 1) * size), mixing_ref[kernel, v, w], factor)
        return local * factor

    for kernel in range(kernels):
        row, column = places((LANES, LANES))
        across_ref[:LANES, lanes_of(kernel)] = filtered(kernel, 0, jnp.abs(row - column))
        gap = jnp.where(row < LANES // 2, LANES + row - column, LANES - row + column)
        across_ref[LANES:, lanes_of(kernel)] = filtered(kernel, 0, gap)
        step = downward_ref.shape[1] // variables
        tall = step + 2 * half
        row, column = places((step, variables * tall))
        local = filtered(kernel, 1, jnp.abs((column & (tall - 1)) - half - row)).astype(F32)
        for v in range(variables):
            halves(downward_ref, kernel, v * step, mixed(kernel, local, v, column, tall))
        size = 2 * half
        row, column = places((size, variables * size))
        bits = half.bit_length() - 1
        i, h = row & (half - 1), column & (half - 1)
        which = (row >> bits) & 1
        gap = jnp.where((which == 0) == swapped, i - h, h - i)
        reach = (gap <= 0) & (which == ((column >> bits) & 1))
        local = filtered(kernel, 1, jnp.where(reach, gap + half, -1)).astype(F32)
        for v in range(variables):
            halves(fringe_ref, kernel, v * size, mixed(kernel, local, v, column, size))


def prepare(probes, taps, mixing, span, half):
    count, variables, rows, cols = probes.shape
    kernels = taps.shape[0]
    planes, tiles = count * variables, cols // LANES
    size = 2 * half * variables
    strip = jax.ShapeDtypeStruct((planes + 1, tiles, half, LANES), BF16)
    outs = (
        jax.ShapeDtypeStruct((planes, tiles, rows, LANES), BF16),
        strip,
        strip,
        jax.ShapeDtypeStruct((tiles, rows, LANES), BF16),
        jax.ShapeDtypeStruct((2 * LANES, kernels * LANES), BF16),
        jax.ShapeDtypeStruct((kernels, 2 * LANES - 2 * half * variables, PARTS * 2 * LANES), BF16),
        jax.ShapeDtypeStruct((kernels, size, PARTS * size), BF16),
    )
    return pl.pallas_call(
        functools.partial(prepare_kernel, half),
        grid=(count,),
        out_shape=outs,
        in_specs=[SMEM, SMEM, whole(span), pl.BlockSpec((1, *probes.shape[1:]), lambda p: (p, 0, 0, 0))],
        out_specs=tuple(whole(o) for o in outs),
        cost_estimate=pl.CostEstimate(flops=10**7, bytes_accessed=4 << 20, transcendentals=0),
        compiler_params=pltpu.CompilerParams(vmem_limit_bytes=16 << 20),
        name="prepare",
    )(taps, mixing, span, probes)


def corner_kernel(inner_ref, outer_ref, near_in, far_in, near_ref, far_ref):
    tiles, half = near_ref.shape[1:3]
    groups, rows, _ = inner_ref.shape
    swapped = odd("band")
    for at, ref in ((0, inner_ref), (groups, outer_ref)):
        for group in range(groups):
            up, down = ref[group, :half], ref[group, rows - half :]
            near_ref[0, at + group] = jnp.where(swapped, up, down)
            far_ref[0, at + group] = jnp.where(swapped, down, up)
    for tile in range(2 * groups, tiles):
        near_ref[0, tile] = jnp.zeros_like(near_ref[0, tile])
        far_ref[0, tile] = jnp.zeros_like(far_ref[0, tile])


def corner(inner, outer, near, far):
    last = pl.BlockSpec((1, *near.shape[1:]), lambda _: (near.shape[0] - 1, 0, 0, 0))
    keep = pl.BlockSpec(memory_space=pl.ANY)
    return pl.pallas_call(
        corner_kernel,
        grid=(1,),
        out_shape=(jax.ShapeDtypeStruct(near.shape, BF16),) * 2,
        in_specs=[whole(inner), whole(outer), keep, keep],
        out_specs=(last, last),
        input_output_aliases={2: 0, 3: 1},
        compiler_params=pltpu.CompilerParams(vmem_limit_bytes=16 << 20),
        name="corner",
    )(inner, outer, near, far)


def around(tile_of, v, tile, tiles, west, east, probe, half, variables):
    slot = (probe % (LANES // half // variables)) * variables + v

    def line_up(block, lane):
        return pltpu.roll(block.astype(F32), (lane + LANES - half * slot) % LANES, 1).astype(BF16)

    before = tile_of(v, tile - 1) if tile > 0 else line_up(west, LANES - half)
    after = tile_of(v, tile + 1) if tile + 1 < tiles else line_up(east, 0)
    lane = lax.broadcasted_iota(jnp.int32, before.shape, 1)
    return jnp.where(lane < LANES // 2, after, before)


def fold(part):
    height, width = part.shape
    folded = jnp.sum(part.reshape(height // 8, 8, width), axis=0)
    return sum(folded[:, lanes_of(t)] for t in range(width // LANES))


def own_kernel(
    half,
    nugget_ref,
    across_ref,
    downward_ref,
    masked_ref,
    land_ref,
    inner_ref,
    outer_ref,
    out_ref,
    edge_ref,
    sums_ref,
    interior_ref,
):
    probe = pl.program_id(0)
    variables, rows, cols = out_ref.shape[1:]
    kernels = downward_ref.shape[0]
    tiles = cols // LANES
    upper = jnp.where(odd("band"), 0, 1)

    @pl.when(probe == 0)
    def _():
        for first in (0, half + rows):
            blank = (slice(None),) * 3 + (slice(first, first + half), slice(None))
            interior_ref[blank] = jnp.zeros_like(interior_ref[blank])

    group = probe // (LANES // half // variables)
    swapped = odd("region")
    inner, outer = inner_ref[group], outer_ref[group]

    west, east = jnp.where(swapped, inner, outer), jnp.where(swapped, outer, inner)

    def tile_of(v, tile):
        return masked_ref[probe * variables + v, tile]

    sums = [jnp.zeros((8, LANES), F32) for _ in range(kernels + 1)]
    wide = 2 * LANES
    step = downward_ref.shape[1] // variables
    parts = downward_ref.shape[2] // wide

    def filter_columns(chunk):
        for tile in (2 * chunk, 2 * chunk + 1):
            window = []
            for v in range(variables):
                sides = around(tile_of, v, tile, tiles, west, east, probe, half, variables)
                window.append(jnp.concatenate([tile_of(v, tile), sides], axis=1))
            window = jnp.concatenate(window, axis=0)
            both = jnp.dot(window, across_ref[...], preferred_element_type=F32).astype(BF16)
            for kernel in range(kernels):
                interior_ref[kernel, :, tile, half : half + rows] = both[:, lanes_of(kernel)].reshape(
                    variables, rows, LANES
                )

    def filter_rows(chunk):
        span = slice(chunk * wide, (chunk + 1) * wide)
        for first in range(0, rows, step):
            here = slice(first, first + step)
            terms = []
            for kernel in range(kernels):
                window = jnp.concatenate(
                    [
                        interior_ref[kernel, :, tile, first : first + step + 2 * half].reshape(wide, LANES)
                        for tile in (2 * chunk, 2 * chunk + 1)
                    ],
                    axis=1,
                )
                window = jnp.concatenate([window] * parts, axis=0)
                terms.append(jnp.dot(downward_ref[kernel], window, preferred_element_type=F32))
            land = jnp.concatenate([land_ref[2 * chunk, here], land_ref[2 * chunk + 1, here]], axis=1)
            for v in range(variables):
                plane = probe * variables + v
                local = jnp.concatenate(
                    [masked_ref[plane, 2 * chunk, here], masked_ref[plane, 2 * chunk + 1, here]], axis=1
                ).astype(F32)
                total = nugget_ref[v] * local
                sums[kernels] = sums[kernels] + fold(total * local)
                for kernel in range(kernels):
                    term = terms[kernel][v * step : (v + 1) * step]
                    sums[kernel] = sums[kernel] + fold(term * local)
                    total = total + term
                out_ref[0, v, here, span] = total.astype(BF16) * land
                if first == 0:
                    edge_ref[0, v, upper, :, span] = total[:half]
                if first + step == rows:
                    edge_ref[0, v, 1 - upper, :, span] = total[step - half :]

    filter_columns(0)
    for chunk in range(cols // wide):
        if chunk + 1 < cols // wide:
            filter_columns(chunk + 1)
        filter_rows(chunk)
    for k in range(kernels + 1):
        sums_ref[0, k] = sums[k]


def own(nugget, across, downward, masked, land, inner, outer, half, shape):
    count, variables, rows, cols = shape
    kernels = downward.shape[0]
    block = lambda *shape: pl.BlockSpec((1, *shape), lambda p: (p,) + (0,) * len(shape))
    outs = (
        jax.ShapeDtypeStruct(shape, BF16),
        jax.ShapeDtypeStruct((count, variables, 2, half, cols), F32),
        jax.ShapeDtypeStruct((count, kernels + 1, 8, LANES), F32),
    )
    operands = (across, downward, masked, land, inner, outer)
    return pl.pallas_call(
        functools.partial(own_kernel, half),
        grid=(count,),
        out_shape=outs,
        in_specs=[SMEM] + [whole(o) for o in operands],
        out_specs=tuple(block(*o.shape[1:]) for o in outs),
        scratch_shapes=[pltpu.VMEM((kernels, variables, cols // LANES, rows + 2 * half, LANES), BF16)],
        cost_estimate=pl.CostEstimate(flops=10**10, bytes_accessed=16 << 20, transcendentals=0),
        compiler_params=pltpu.CompilerParams(vmem_limit_bytes=32 << 20),
        name="own",
    )(nugget, *operands)


def border_kernel(
    half,
    across_ref,
    fringe_ref,
    land_ref,
    near_ref,
    far_ref,
    near_own_ref,
    far_own_ref,
    edge_ref,
    sums_ref,
    base_ref,
    out_ref,
    quad_ref,
    ready_ref,
    total_ref,
    sem,
):
    count, variables, _, _, cols = edge_ref.shape
    rows = out_ref.shape[2]
    shares = sums_ref.shape[1]
    kernels = shares - 1
    tiles = cols // LANES
    per_group = LANES // half // variables
    groups = count // per_group
    flipped = odd("region")
    upper = jnp.where(odd("band"), 0, rows - half)
    firsts = [pl.multiple_of(upper, half), pl.multiple_of(rows - half - upper, half)]
    size = 2 * half * variables
    wide = 2 * LANES
    last = count * variables

    halos = (near_ref, far_ref)

    def corners(ref, p):
        inner, outer = (ref[last, kind + p // per_group] for kind in (0, groups))
        return jnp.where(flipped, inner, outer), jnp.where(flipped, outer, inner)

    ends = {(at, p): corners(halos[at], p) for at in range(2) for p in range(count)}

    def filter_columns(tile):
        window = []
        for p in range(count):
            for v in range(variables):
                for at in range(2):
                    tile_of = lambda v, t: halos[at][p * variables + v, t]
                    sides = around(tile_of, v, tile, tiles, *ends[at, p], p, half, variables)
                    window.append(jnp.concatenate([tile_of(v, tile), sides], axis=1))
        window = jnp.concatenate(window, axis=0)
        both = jnp.dot(window, across_ref[...], preferred_element_type=F32).astype(BF16)
        for kernel in range(kernels):
            piece = both[:, lanes_of(kernel)].reshape(count, size, LANES)
            ready_ref[kernel, :, tile] = piece

    sums = {(p, k): sums_ref[p, k] for p in range(count) for k in range(shares)}

    def filter_rows(chunk):
        span = slice(chunk * wide, (chunk + 1) * wide)
        pair = (2 * chunk, 2 * chunk + 1)
        strips = [
            jnp.concatenate([land_ref[tile, pl.ds(first, half)] for tile in pair], axis=1) for first in firsts
        ]
        shore = jnp.stack(strips)
        for p in range(count):
            planes = slice(p * variables, (p + 1) * variables)
            near, far = (
                jnp.concatenate([ref[planes, tile] for tile in pair], axis=2) for ref in (near_own_ref, far_own_ref)
            )
            total = edge_ref[p, :, :, :, span]
            local = jnp.stack([near, far], axis=1).astype(F32)
            for kernel in range(kernels):
                window = jnp.concatenate([ready_ref[kernel, p, tile] for tile in pair], axis=1)
                window = jnp.concatenate([window] * (fringe_ref.shape[2] // size), axis=0)
                term = jnp.dot(fringe_ref[kernel], window, preferred_element_type=F32)
                sums[p, kernel] = sums[p, kernel] + fold(term * local.reshape(size, wide))
                total = total + term.reshape(total.shape)
            total_ref[p, :, :, :, span] = total.astype(BF16) * shore[None]

    chunks = cols // wide
    for tile in (0, 1):
        filter_columns(tile)
    for chunk in range(chunks):
        for tile in (2 * chunk + 2, 2 * chunk + 3):
            if tile < tiles:
                filter_columns(tile)
        filter_rows(chunk)

    copies = [
        pltpu.make_async_copy(total_ref.at[:, :, at], out_ref.at[:, :, pl.ds(first, half), :], sem.at[at])
        for at, first in enumerate(firsts)
    ]
    for copy in copies:
        copy.start()

    lane = lax.broadcasted_iota(jnp.int32, quad_ref.shape, 1)
    line = jnp.zeros(quad_ref.shape, F32)
    for (p, k), part in sums.items():
        line = jnp.where(lane == p * shares + k, jnp.sum(part), line)
    quad_ref[...] = line
    for copy in copies:
        copy.wait()


def border(across, fringe, land, near, far, near_own, far_own, edge, sums, base, half, devices):
    count, variables, _, cols = base.shape
    kernels = fringe.shape[0]
    size = 2 * half * variables
    keep = pl.BlockSpec(memory_space=pl.ANY)
    quads = jax.ShapeDtypeStruct((devices, LANES), F32)
    operands = (across, fringe, land, near, far, near_own, far_own, edge, sums)
    return pl.pallas_call(
        functools.partial(border_kernel, half),
        grid=(1,),
        out_shape=(jax.ShapeDtypeStruct(base.shape, BF16), quads),
        in_specs=[whole(o) for o in operands] + [keep],
        out_specs=(keep, whole(quads)),
        scratch_shapes=[
            pltpu.VMEM((kernels, count, cols // LANES, size, LANES), BF16),
            pltpu.VMEM((count, variables, 2, half, cols), BF16),
            pltpu.SemaphoreType.DMA((2,)),
        ],
        input_output_aliases={len(operands): 0},
        compiler_params=pltpu.CompilerParams(vmem_limit_bytes=32 << 20),
        name="border",
    )(*operands, base)


def per_device(probes, filter_taps, mixing, nugget, land_span):
    count, _, rows, cols = probes.shape
    kernels = filter_taps.shape[0]
    half = filter_taps.shape[2] - 1
    regions, bands = lax.axis_size("region"), lax.axis_size("band")
    inner_pairs = [(i, i ^ 1) for i in range(regions)]
    outer_pairs = [(i, (i + 1 if i % 2 else i - 1) % regions) for i in range(regions)]
    near_pairs = [(i, i ^ 1) for i in range(bands)]
    far_pairs = [(i, i + 1 if i % 2 else i - 1) for i in range(1, bands - 1)]

    probes = pltpu.with_memory_space_constraint(probes, pltpu.HBM)
    span = pltpu.with_memory_space_constraint(land_span.reshape(2, 1, rows), pltpu.HBM)
    inner, outer = pack(probes, span, half)
    outer = lax.ppermute(outer, "region", outer_pairs)
    inner = lax.ppermute(inner, "region", inner_pairs)
    masked, near, far, land, across, downward, fringe = prepare(probes, filter_taps, mixing, span, half)
    near, far = corner(inner, outer, near, far)
    near_halo = lax.ppermute(near, "band", near_pairs)
    far_halo = lax.ppermute(far, "band", far_pairs)
    base, edge, sums = own(nugget, across, downward, masked, land, inner, outer, half, probes.shape)
    output, quads = border(
        across, fringe, land, near_halo, far_halo, near, far, edge, sums, base, half, regions * bands
    )
    shares = lax.all_to_all(quads, ("region", "band"), 0, 0, tiled=True)
    quadratic = jnp.sum(shares, axis=0)[: count * (kernels + 1)].reshape(count, kernels + 1)
    return output, quadratic / (bands * rows * cols)


def solution(mesh):
    in_specs = (P(None, None, "band", "region"), P(), P(), P(), P(None, "band", "region"))
    out_specs = (P(None, None, "band", "region"), P())
    return jax.shard_map(
        per_device, mesh=mesh, in_specs=in_specs, out_specs=out_specs, check_vma=False
    )
```

```python
import functools

import jax
import jax.numpy as jnp
from jax import lax
from jax.experimental import pallas as pl
from jax.experimental.pallas import tpu as pltpu
from jax.sharding import PartitionSpec as P

LANES = 128
BF16 = jnp.bfloat16
F32 = jnp.float32
PARTS = 1
SMEM = pl.BlockSpec(memory_space=pltpu.SMEM)


def lanes_of(tile):
    return slice(tile * LANES, (tile + 1) * LANES)


def whole(a):
    return pl.BlockSpec(a.shape, lambda *_: (0,) * len(a.shape))


def odd(axis):
    return lax.axis_index(axis) % 2 != 0


def bounds_by_row(span_ref):
    return [jnp.broadcast_to(span_ref[entry].astype(F32), (LANES, LANES)).T for entry in range(2)]


def land_tile(low, high, first_col):
    column = (lax.broadcasted_iota(jnp.int32, low.shape, 1) + first_col).astype(F32)
    return ((column >= low) & (column < high)).astype(F32).astype(BF16)


def pack_kernel(half, cols, span_ref, west_ref, east_ref, inner_ref, outer_ref):
    variables = west_ref.shape[1]
    per_group = LANES // half
    swapped = odd("region")
    low, high = bounds_by_row(span_ref)
    lane = lax.broadcasted_iota(jnp.int32, low.shape, 1)
    column = (lane & (half - 1)).astype(F32)
    first = ((column >= low) & (column < high)).astype(F32).astype(BF16)
    column = column + (cols - half)
    last = ((column >= low) & (column < high)).astype(F32).astype(BF16)
    for group in range(inner_ref.shape[0]):
        left = right = None
        for k in range(per_group + 1):
            plane = group * per_group + k
            west = west_ref[plane // variables, plane % variables] if k < per_group else None
            plane -= 1
            east = east_ref[plane // variables, plane % variables] if k > 0 else None
            if east is None:
                both = west
            elif west is None:
                both = east
            else:
                both = jnp.where(lane < LANES // 2, west, east)
                both = pltpu.roll(both, k * half, 1)
            if west is not None:
                left = both if left is None else jnp.where(lane < k * half, left, both)
            if east is not None:
                right = both if right is None else jnp.where(lane < (k - 1) * half, right, both)
        left, right = left * first, right * last
        inner_ref[group] = jnp.where(swapped, left, right)
        outer_ref[group] = jnp.where(swapped, right, left)


def pack(probes, span, half):
    count, variables, rows, cols = probes.shape
    groups = count * variables * half // LANES
    steps = 1
    edge = jax.ShapeDtypeStruct((groups, rows, LANES), BF16)
    tile = lambda at: pl.BlockSpec((count // steps, variables, rows, LANES), lambda g: (g, 0, 0, at))
    piece = pl.BlockSpec((groups // steps, rows, LANES), lambda g: (g, 0, 0))
    return pl.pallas_call(
        functools.partial(pack_kernel, half, cols),
        grid=(steps,),
        out_shape=(edge, edge),
        in_specs=[whole(span), tile(0), tile(cols // LANES - 1)],
        out_specs=(piece, piece),
        compiler_params=pltpu.CompilerParams(vmem_limit_bytes=16 << 20),
        name="pack",
    )(span, probes, probes)


def prepare_kernel(
    half,
    taps_ref,
    mixing_ref,
    span_ref,
    x_ref,
    masked_ref,
    near_ref,
    far_ref,
    land_ref,
    across_ref,
    downward_ref,
    fringe_ref,
):
    probe = pl.program_id(0)
    variables, rows, cols = x_ref.shape[1:]
    tiles = cols // LANES
    swapped = odd("band")

    @pl.when(probe == 0)
    def _():
        low, high = bounds_by_row(span_ref)
        for tile in range(tiles):
            land_ref[tile] = land_tile(low, high, tile * LANES)

    for tile in range(tiles):
        land = land_ref[tile]
        for v in range(variables):
            plane = probe * variables + v
            value = x_ref[0, v, :, lanes_of(tile)] * land
            masked_ref[plane, tile] = value
            up, down = value[:half], value[rows - half :]
            near_ref[plane, tile] = jnp.where(swapped, up, down)
            far_ref[plane, tile] = jnp.where(swapped, down, up)

    @pl.when(probe == pl.num_programs(0) - 1)
    def _():
        make_tables(half, variables, taps_ref, mixing_ref, across_ref, downward_ref, fringe_ref)


def make_tables(half, variables, taps_ref, mixing_ref, across_ref, downward_ref, fringe_ref):
    kernels = downward_ref.shape[0]
    swapped = odd("band")

    def filtered(kernel, which, distance):
        table = jnp.zeros(distance.shape, F32)
        for tap in range(half + 1):
            table = jnp.where(distance == tap, taps_ref[kernel, which, tap], table)
        return table.astype(BF16)

    def places(shape):
        return lax.broadcasted_iota(jnp.int32, shape, 0), lax.broadcasted_iota(jnp.int32, shape, 1)

    def halves(ref, kernel, first, weight):
        height, width = weight.shape
        parts = ref.shape[2] // width
        for part in range(parts):
            piece = weight.astype(BF16)
            ref[kernel, first : first + height, part * width : (part + 1) * width] = piece
            weight = weight - piece.astype(F32)

    def mixed(kernel, local, v, column, size):
        factor = jnp.zeros(local.shape, F32)
        for w in range(variables):
            factor = jnp.where((column >= w * size) & (column < (w + 1) * size), mixing_ref[kernel, v, w], factor)
        return local * factor

    for kernel in range(kernels):
        row, column = places((LANES, LANES))
        across_ref[:LANES, lanes_of(kernel)] = filtered(kernel, 0, jnp.abs(row - column))
        gap = jnp.where(row < LANES // 2, LANES + row - column, LANES - row + column)
        across_ref[LANES:, lanes_of(kernel)] = filtered(kernel, 0, gap)
        step = downward_ref.shape[1] // variables
        tall = step + 2 * half
        row, column = places((step, variables * tall))
        local = filtered(kernel, 1, jnp.abs((column & (tall - 1)) - half - row)).astype(F32)
        for v in range(variables):
            halves(downward_ref, kernel, v * step, mixed(kernel, local, v, column, tall))
        size = 2 * half
        row, column = places((size, variables * size))
        bits = half.bit_length() - 1
        i, h = row & (half - 1), column & (half - 1)
        which = (row >> bits) & 1
        gap = jnp.where((which == 0) == swapped, i - h, h - i)
        reach = (gap <= 0) & (which == ((column >> bits) & 1))
        local = filtered(kernel, 1, jnp.where(reach, gap + half, -1)).astype(F32)
        for v in range(variables):
            halves(fringe_ref, kernel, v * size, mixed(kernel, local, v, column, size))


def prepare(probes, taps, mixing, span, half):
    count, variables, rows, cols = probes.shape
    kernels = taps.shape[0]
    planes, tiles = count * variables, cols // LANES
    size = 2 * half * variables
    strip = jax.ShapeDtypeStruct((planes + 1, tiles, half, LANES), BF16)
    outs = (
        jax.ShapeDtypeStruct((planes, tiles, rows, LANES), BF16),
        strip,
        strip,
        jax.ShapeDtypeStruct((tiles, rows, LANES), BF16),
        jax.ShapeDtypeStruct((2 * LANES, kernels * LANES), BF16),
        jax.ShapeDtypeStruct((kernels, 2 * LANES - 2 * half * variables, PARTS * 2 * LANES), BF16),
        jax.ShapeDtypeStruct((kernels, size, PARTS * size), BF16),
    )
    return pl.pallas_call(
        functools.partial(prepare_kernel, half),
        grid=(count,),
        out_shape=outs,
        in_specs=[SMEM, SMEM, whole(span), pl.BlockSpec((1, *probes.shape[1:]), lambda p: (p, 0, 0, 0))],
        out_specs=tuple(whole(o) for o in outs),
        cost_estimate=pl.CostEstimate(flops=10**7, bytes_accessed=4 << 20, transcendentals=0),
        compiler_params=pltpu.CompilerParams(vmem_limit_bytes=16 << 20),
        name="prepare",
    )(taps, mixing, span, probes)


def corner_kernel(inner_ref, outer_ref, near_in, far_in, near_ref, far_ref):
    tiles, half = near_ref.shape[1:3]
    groups, rows, _ = inner_ref.shape
    swapped = odd("band")
    for at, ref in ((0, inner_ref), (groups, outer_ref)):
        for group in range(groups):
            up, down = ref[group, :half], ref[group, rows - half :]
            near_ref[0, at + group] = jnp.where(swapped, up, down)
            far_ref[0, at + group] = jnp.where(swapped, down, up)
    for tile in range(2 * groups, tiles):
        near_ref[0, tile] = jnp.zeros_like(near_ref[0, tile])
        far_ref[0, tile] = jnp.zeros_like(far_ref[0, tile])


def corner(inner, outer, near, far):
    last = pl.BlockSpec((1, *near.shape[1:]), lambda _: (near.shape[0] - 1, 0, 0, 0))
    keep = pl.BlockSpec(memory_space=pl.ANY)
    return pl.pallas_call(
        corner_kernel,
        grid=(1,),
        out_shape=(jax.ShapeDtypeStruct(near.shape, BF16),) * 2,
        in_specs=[whole(inner), whole(outer), keep, keep],
        out_specs=(last, last),
        input_output_aliases={2: 0, 3: 1},
        compiler_params=pltpu.CompilerParams(vmem_limit_bytes=16 << 20),
        name="corner",
    )(inner, outer, near, far)


def around(tile_of, v, tile, tiles, west, east, probe, half, variables):
    slot = (probe % (LANES // half // variables)) * variables + v

    def line_up(block, lane):
        return pltpu.roll(block.astype(F32), (lane + LANES - half * slot) % LANES, 1).astype(BF16)

    before = tile_of(v, tile - 1) if tile > 0 else line_up(west, LANES - half)
    after = tile_of(v, tile + 1) if tile + 1 < tiles else line_up(east, 0)
    lane = lax.broadcasted_iota(jnp.int32, before.shape, 1)
    return jnp.where(lane < LANES // 2, after, before)


def fold(part):
    height, width = part.shape
    folded = jnp.sum(part.reshape(height // 8, 8, width), axis=0)
    return sum(folded[:, lanes_of(t)] for t in range(width // LANES))


def own_kernel(
    half,
    nugget_ref,
    across_ref,
    downward_ref,
    masked_ref,
    land_ref,
    inner_ref,
    outer_ref,
    out_ref,
    edge_ref,
    sums_ref,
    interior_ref,
):
    probe = pl.program_id(0)
    variables, rows, cols = out_ref.shape[1:]
    kernels = downward_ref.shape[0]
    tiles = cols // LANES
    upper = jnp.where(odd("band"), 0, 1)

    @pl.when(probe == 0)
    def _():
        for first in (0, half + rows):
            blank = (slice(None),) * 3 + (slice(first, first + half), slice(None))
            interior_ref[blank] = jnp.zeros_like(interior_ref[blank])

    group = probe // (LANES // half // variables)
    swapped = odd("region")
    inner, outer = inner_ref[group], outer_ref[group]

    west, east = jnp.where(swapped, inner, outer), jnp.where(swapped, outer, inner)

    def tile_of(v, tile):
        return masked_ref[probe * variables + v, tile]

    sums = [jnp.zeros((8, LANES), F32) for _ in range(kernels + 1)]
    wide = 2 * LANES
    step = downward_ref.shape[1] // variables
    parts = downward_ref.shape[2] // wide

    def filter_columns(chunk):
        for tile in (2 * chunk, 2 * chunk + 1):
            window = []
            for v in range(variables):
                sides = around(tile_of, v, tile, tiles, west, east, probe, half, variables)
                window.append(jnp.concatenate([tile_of(v, tile), sides], axis=1))
            window = jnp.concatenate(window, axis=0)
            both = jnp.dot(window, across_ref[...], preferred_element_type=F32).astype(BF16)
            for kernel in range(kernels):
                interior_ref[kernel, :, tile, half : half + rows] = both[:, lanes_of(kernel)].reshape(
                    variables, rows, LANES
                )

    def filter_rows(chunk):
        span = slice(chunk * wide, (chunk + 1) * wide)
        for first in range(0, rows, step):
            here = slice(first, first + step)
            terms = []
            for kernel in range(kernels):
                window = jnp.concatenate(
                    [
                        interior_ref[kernel, :, tile, first : first + step + 2 * half].reshape(wide, LANES)
                        for tile in (2 * chunk, 2 * chunk + 1)
                    ],
                    axis=1,
                )
                window = jnp.concatenate([window] * parts, axis=0)
                terms.append(jnp.dot(downward_ref[kernel], window, preferred_element_type=F32))
            land = jnp.concatenate([land_ref[2 * chunk, here], land_ref[2 * chunk + 1, here]], axis=1)
            for v in range(variables):
                plane = probe * variables + v
                local = jnp.concatenate(
                    [masked_ref[plane, 2 * chunk, here], masked_ref[plane, 2 * chunk + 1, here]], axis=1
                ).astype(F32)
                total = nugget_ref[v] * local
                sums[kernels] = sums[kernels] + fold(total * local)
                for kernel in range(kernels):
                    term = terms[kernel][v * step : (v + 1) * step]
                    sums[kernel] = sums[kernel] + fold(term * local)
                    total = total + term
                out_ref[0, v, here, span] = total.astype(BF16) * land
                if first == 0:
                    edge_ref[probe, v, upper, :, span] = total[:half]
                if first + step == rows:
                    edge_ref[probe, v, 1 - upper, :, span] = total[step - half :]

    filter_columns(0)
    for chunk in range(cols // wide):
        if chunk + 1 < cols // wide:
            filter_columns(chunk + 1)
        filter_rows(chunk)
    for k in range(kernels + 1):
        sums_ref[probe, k] = sums[k]


def own(nugget, across, downward, masked, land, inner, outer, half, shape):
    count, variables, rows, cols = shape
    kernels = downward.shape[0]
    block = lambda *shape: pl.BlockSpec((1, *shape), lambda p: (p,) + (0,) * len(shape))
    outs = (
        jax.ShapeDtypeStruct(shape, BF16),
        jax.ShapeDtypeStruct((count, variables, 2, half, cols), F32),
        jax.ShapeDtypeStruct((count, kernels + 1, 8, LANES), F32),
    )
    operands = (across, downward, masked, land, inner, outer)
    return pl.pallas_call(
        functools.partial(own_kernel, half),
        grid=(count,),
        out_shape=outs,
        in_specs=[SMEM] + [whole(o) for o in operands],
        out_specs=(block(*shape[1:]), whole(outs[1]), whole(outs[2])),
        scratch_shapes=[pltpu.VMEM((kernels, variables, cols // LANES, rows + 2 * half, LANES), BF16)],
        cost_estimate=pl.CostEstimate(flops=10**10, bytes_accessed=16 << 20, transcendentals=0),
        compiler_params=pltpu.CompilerParams(vmem_limit_bytes=32 << 20),
        name="own",
    )(nugget, *operands)


def border_kernel(
    half,
    across_ref,
    fringe_ref,
    land_ref,
    near_ref,
    far_ref,
    near_own_ref,
    far_own_ref,
    edge_ref,
    sums_ref,
    base_ref,
    out_ref,
    quad_ref,
    ready_ref,
    total_ref,
    sem,
):
    count, variables, _, _, cols = edge_ref.shape
    rows = out_ref.shape[2]
    shares = sums_ref.shape[1]
    kernels = shares - 1
    tiles = cols // LANES
    per_group = LANES // half // variables
    groups = count // per_group
    flipped = odd("region")
    upper = jnp.where(odd("band"), 0, rows - half)
    firsts = [pl.multiple_of(upper, half), pl.multiple_of(rows - half - upper, half)]
    size = 2 * half * variables
    wide = 2 * LANES
    last = count * variables

    halos = (near_ref, far_ref)

    def corners(ref, p):
        inner, outer = (ref[last, kind + p // per_group] for kind in (0, groups))
        return jnp.where(flipped, inner, outer), jnp.where(flipped, outer, inner)

    ends = {(at, p): corners(halos[at], p) for at in range(2) for p in range(count)}

    def filter_columns(tile):
        window = []
        for p in range(count):
            for v in range(variables):
                for at in range(2):
                    tile_of = lambda v, t: halos[at][p * variables + v, t]
                    sides = around(tile_of, v, tile, tiles, *ends[at, p], p, half, variables)
                    window.append(jnp.concatenate([tile_of(v, tile), sides], axis=1))
        window = jnp.concatenate(window, axis=0)
        both = jnp.dot(window, across_ref[...], preferred_element_type=F32).astype(BF16)
        for kernel in range(kernels):
            piece = both[:, lanes_of(kernel)].reshape(count, size, LANES)
            ready_ref[kernel, :, tile] = piece

    sums = {(p, k): sums_ref[p, k] for p in range(count) for k in range(shares)}

    def filter_rows(chunk):
        span = slice(chunk * wide, (chunk + 1) * wide)
        pair = (2 * chunk, 2 * chunk + 1)
        strips = [
            jnp.concatenate([land_ref[tile, pl.ds(first, half)] for tile in pair], axis=1) for first in firsts
        ]
        shore = jnp.stack(strips)
        for p in range(count):
            planes = slice(p * variables, (p + 1) * variables)
            near, far = (
                jnp.concatenate([ref[planes, tile] for tile in pair], axis=2) for ref in (near_own_ref, far_own_ref)
            )
            total = edge_ref[p, :, :, :, span]
            local = jnp.stack([near, far], axis=1).astype(F32)
            for kernel in range(kernels):
                window = jnp.concatenate([ready_ref[kernel, p, tile] for tile in pair], axis=1)
                window = jnp.concatenate([window] * (fringe_ref.shape[2] // size), axis=0)
                term = jnp.dot(fringe_ref[kernel], window, preferred_element_type=F32)
                sums[p, kernel] = sums[p, kernel] + fold(term * local.reshape(size, wide))
                total = total + term.reshape(total.shape)
            total_ref[p, :, :, :, span] = total.astype(BF16) * shore[None]

    chunks = cols // wide
    for tile in (0, 1):
        filter_columns(tile)
    for chunk in range(chunks):
        for tile in (2 * chunk + 2, 2 * chunk + 3):
            if tile < tiles:
                filter_columns(tile)
        filter_rows(chunk)

    copies = [
        pltpu.make_async_copy(total_ref.at[:, :, at], out_ref.at[:, :, pl.ds(first, half), :], sem.at[at])
        for at, first in enumerate(firsts)
    ]
    for copy in copies:
        copy.start()

    lane = lax.broadcasted_iota(jnp.int32, quad_ref.shape, 1)
    line = jnp.zeros(quad_ref.shape, F32)
    for (p, k), part in sums.items():
        line = jnp.where(lane == p * shares + k, jnp.sum(part), line)
    quad_ref[...] = line
    for copy in copies:
        copy.wait()


def border(across, fringe, land, near, far, near_own, far_own, edge, sums, base, half, devices):
    count, variables, _, cols = base.shape
    kernels = fringe.shape[0]
    size = 2 * half * variables
    keep = pl.BlockSpec(memory_space=pl.ANY)
    quads = jax.ShapeDtypeStruct((devices, LANES), F32)
    operands = (across, fringe, land, near, far, near_own, far_own, edge, sums)
    return pl.pallas_call(
        functools.partial(border_kernel, half),
        grid=(1,),
        out_shape=(jax.ShapeDtypeStruct(base.shape, BF16), quads),
        in_specs=[whole(o) for o in operands] + [keep],
        out_specs=(keep, whole(quads)),
        scratch_shapes=[
            pltpu.VMEM((kernels, count, cols // LANES, size, LANES), BF16),
            pltpu.VMEM((count, variables, 2, half, cols), BF16),
            pltpu.SemaphoreType.DMA((2,)),
        ],
        input_output_aliases={len(operands): 0},
        compiler_params=pltpu.CompilerParams(vmem_limit_bytes=32 << 20),
        name="border",
    )(*operands, base)


def per_device(probes, filter_taps, mixing, nugget, land_span):
    count, _, rows, cols = probes.shape
    kernels = filter_taps.shape[0]
    half = filter_taps.shape[2] - 1
    regions, bands = lax.axis_size("region"), lax.axis_size("band")
    inner_pairs = [(i, i ^ 1) for i in range(regions)]
    outer_pairs = [(i, (i + 1 if i % 2 else i - 1) % regions) for i in range(regions)]
    near_pairs = [(i, i ^ 1) for i in range(bands)]
    far_pairs = [(i, i + 1 if i % 2 else i - 1) for i in range(1, bands - 1)]

    probes = pltpu.with_memory_space_constraint(probes, pltpu.HBM)
    span = pltpu.with_memory_space_constraint(land_span.reshape(2, 1, rows), pltpu.HBM)
    inner, outer = pack(probes, span, half)
    outer = lax.ppermute(outer, "region", outer_pairs)
    inner = lax.ppermute(inner, "region", inner_pairs)
    masked, near, far, land, across, downward, fringe = prepare(probes, filter_taps, mixing, span, half)
    near, far = corner(inner, outer, near, far)
    near_halo = lax.ppermute(near, "band", near_pairs)
    far_halo = lax.ppermute(far, "band", far_pairs)
    base, edge, sums = own(nugget, across, downward, masked, land, inner, outer, half, probes.shape)
    output, quads = border(
        across, fringe, land, near_halo, far_halo, near, far, edge, sums, base, half, regions * bands
    )
    shares = lax.all_to_all(quads, ("region", "band"), 0, 0, tiled=True)
    quadratic = jnp.sum(shares, axis=0)[: count * (kernels + 1)].reshape(count, kernels + 1)
    return output, quadratic / (bands * rows * cols)


def solution(mesh):
    in_specs = (P(None, None, "band", "region"), P(), P(), P(), P(None, "band", "region"))
    out_specs = (P(None, None, "band", "region"), P())
    return jax.shard_map(
        per_device, mesh=mesh, in_specs=in_specs, out_specs=out_specs, check_vma=False
    )
```

```python
import functools

import jax
import jax.numpy as jnp
from jax import lax
from jax.experimental import pallas as pl
from jax.experimental.pallas import tpu as pltpu
from jax.sharding import PartitionSpec as P

LANES = 128
BF16 = jnp.bfloat16
F32 = jnp.float32
PARTS = 1
SMEM = pl.BlockSpec(memory_space=pltpu.SMEM)


def lanes_of(tile):
    return slice(tile * LANES, (tile + 1) * LANES)


def whole(a):
    return pl.BlockSpec(a.shape, lambda *_: (0,) * len(a.shape))


def odd(axis):
    return lax.axis_index(axis) % 2 != 0


def bounds_by_row(span_ref):
    return [jnp.broadcast_to(span_ref[entry].astype(F32), (LANES, LANES)).T for entry in range(2)]


def land_tile(low, high, first_col):
    column = (lax.broadcasted_iota(jnp.int32, low.shape, 1) + first_col).astype(F32)
    return ((column >= low) & (column < high)).astype(F32).astype(BF16)


def pack_kernel(half, cols, span_ref, west_ref, east_ref, inner_ref, outer_ref):
    variables = west_ref.shape[1]
    per_group = LANES // half
    swapped = odd("region")
    low, high = bounds_by_row(span_ref)
    lane = lax.broadcasted_iota(jnp.int32, low.shape, 1)
    column = (lane & (half - 1)).astype(F32)
    first = ((column >= low) & (column < high)).astype(F32).astype(BF16)
    column = column + (cols - half)
    last = ((column >= low) & (column < high)).astype(F32).astype(BF16)
    for group in range(inner_ref.shape[0]):
        left = right = None
        for k in range(per_group + 1):
            plane = group * per_group + k
            west = west_ref[plane // variables, plane % variables] if k < per_group else None
            plane -= 1
            east = east_ref[plane // variables, plane % variables] if k > 0 else None
            if east is None:
                both = west
            elif west is None:
                both = east
            else:
                both = jnp.where(lane < LANES // 2, west, east)
                both = pltpu.roll(both, k * half, 1)
            if west is not None:
                left = both if left is None else jnp.where(lane < k * half, left, both)
            if east is not None:
                right = both if right is None else jnp.where(lane < (k - 1) * half, right, both)
        left, right = left * first, right * last
        inner_ref[group] = jnp.where(swapped, left, right)
        outer_ref[group] = jnp.where(swapped, right, left)


def pack(probes, span, half):
    count, variables, rows, cols = probes.shape
    groups = count * variables * half // LANES
    steps = 1
    edge = jax.ShapeDtypeStruct((groups, rows, LANES), BF16)
    tile = lambda at: pl.BlockSpec((count // steps, variables, rows, LANES), lambda g: (g, 0, 0, at))
    piece = pl.BlockSpec((groups // steps, rows, LANES), lambda g: (g, 0, 0))
    return pl.pallas_call(
        functools.partial(pack_kernel, half, cols),
        grid=(steps,),
        out_shape=(edge, edge),
        in_specs=[whole(span), tile(0), tile(cols // LANES - 1)],
        out_specs=(piece, piece),
        compiler_params=pltpu.CompilerParams(vmem_limit_bytes=16 << 20),
        name="pack",
    )(span, probes, probes)


def prepare_kernel(
    half,
    taps_ref,
    mixing_ref,
    span_ref,
    x_ref,
    masked_ref,
    near_ref,
    far_ref,
    land_ref,
    across_ref,
    downward_ref,
    fringe_ref,
):
    probe = pl.program_id(0)
    variables, rows, cols = x_ref.shape[1:]
    tiles = cols // LANES
    swapped = odd("band")

    @pl.when(probe == 0)
    def _():
        low, high = bounds_by_row(span_ref)
        for tile in range(tiles):
            land_ref[tile] = land_tile(low, high, tile * LANES)

    for tile in range(tiles):
        land = land_ref[tile]
        for v in range(variables):
            plane = probe * variables + v
            value = x_ref[0, v, :, lanes_of(tile)] * land
            masked_ref[plane, tile] = value
            up, down = value[:half], value[rows - half :]
            near_ref[plane * tiles + tile] = jnp.where(swapped, up, down)
            far_ref[plane * tiles + tile] = jnp.where(swapped, down, up)

    @pl.when(probe == pl.num_programs(0) - 1)
    def _():
        make_tables(half, variables, taps_ref, mixing_ref, across_ref, downward_ref, fringe_ref)


def make_tables(half, variables, taps_ref, mixing_ref, across_ref, downward_ref, fringe_ref):
    kernels = downward_ref.shape[0]
    swapped = odd("band")

    def filtered(kernel, which, distance):
        table = jnp.zeros(distance.shape, F32)
        for tap in range(half + 1):
            table = jnp.where(distance == tap, taps_ref[kernel, which, tap], table)
        return table.astype(BF16)

    def places(shape):
        return lax.broadcasted_iota(jnp.int32, shape, 0), lax.broadcasted_iota(jnp.int32, shape, 1)

    def halves(ref, kernel, first, weight):
        height, width = weight.shape
        parts = ref.shape[2] // width
        for part in range(parts):
            piece = weight.astype(BF16)
            ref[kernel, first : first + height, part * width : (part + 1) * width] = piece
            weight = weight - piece.astype(F32)

    def mixed(kernel, local, v, column, size):
        factor = jnp.zeros(local.shape, F32)
        for w in range(variables):
            factor = jnp.where((column >= w * size) & (column < (w + 1) * size), mixing_ref[kernel, v, w], factor)
        return local * factor

    for kernel in range(kernels):
        row, column = places((LANES, LANES))
        across_ref[:LANES, lanes_of(kernel)] = filtered(kernel, 0, jnp.abs(row - column))
        gap = jnp.where(row < LANES // 2, LANES + row - column, LANES - row + column)
        across_ref[LANES:, lanes_of(kernel)] = filtered(kernel, 0, gap)
        step = downward_ref.shape[1] // variables
        tall = step + 2 * half
        row, column = places((step, variables * tall))
        local = filtered(kernel, 1, jnp.abs((column & (tall - 1)) - half - row)).astype(F32)
        for v in range(variables):
            halves(downward_ref, kernel, v * step, mixed(kernel, local, v, column, tall))
        size = 2 * half
        row, column = places((size, variables * size))
        bits = half.bit_length() - 1
        i, h = row & (half - 1), column & (half - 1)
        which = (row >> bits) & 1
        gap = jnp.where((which == 0) == swapped, i - h, h - i)
        reach = (gap <= 0) & (which == ((column >> bits) & 1))
        local = filtered(kernel, 1, jnp.where(reach, gap + half, -1)).astype(F32)
        for v in range(variables):
            halves(fringe_ref, kernel, v * size, mixed(kernel, local, v, column, size))


def prepare(probes, taps, mixing, span, half):
    count, variables, rows, cols = probes.shape
    kernels = taps.shape[0]
    planes, tiles = count * variables, cols // LANES
    size = 2 * half * variables
    corners = 2 * planes * half // LANES
    strip = jax.ShapeDtypeStruct((planes * tiles + corners, half, LANES), BF16)
    outs = (
        jax.ShapeDtypeStruct((planes, tiles, rows, LANES), BF16),
        strip,
        strip,
        jax.ShapeDtypeStruct((tiles, rows, LANES), BF16),
        jax.ShapeDtypeStruct((2 * LANES, kernels * LANES), BF16),
        jax.ShapeDtypeStruct((kernels, 2 * LANES - 2 * half * variables, PARTS * 2 * LANES), BF16),
        jax.ShapeDtypeStruct((kernels, size, PARTS * size), BF16),
    )
    return pl.pallas_call(
        functools.partial(prepare_kernel, half),
        grid=(count,),
        out_shape=outs,
        in_specs=[SMEM, SMEM, whole(span), pl.BlockSpec((1, *probes.shape[1:]), lambda p: (p, 0, 0, 0))],
        out_specs=tuple(whole(o) for o in outs),
        cost_estimate=pl.CostEstimate(flops=10**7, bytes_accessed=4 << 20, transcendentals=0),
        compiler_params=pltpu.CompilerParams(vmem_limit_bytes=16 << 20),
        name="prepare",
    )(taps, mixing, span, probes)


def corner_kernel(inner_ref, outer_ref, near_in, far_in, near_ref, far_ref):
    half = near_ref.shape[1]
    groups, rows, _ = inner_ref.shape
    swapped = odd("band")
    for at, ref in ((0, inner_ref), (groups, outer_ref)):
        for group in range(groups):
            up, down = ref[group, :half], ref[group, rows - half :]
            near_ref[at + group] = jnp.where(swapped, up, down)
            far_ref[at + group] = jnp.where(swapped, down, up)


def corner(inner, outer, near, far):
    tiles = 2 * inner.shape[0]
    last = pl.BlockSpec((tiles, *near.shape[1:]), lambda _: (near.shape[0] // tiles - 1, 0, 0))
    keep = pl.BlockSpec(memory_space=pl.ANY)
    return pl.pallas_call(
        corner_kernel,
        grid=(1,),
        out_shape=(jax.ShapeDtypeStruct(near.shape, BF16),) * 2,
        in_specs=[whole(inner), whole(outer), keep, keep],
        out_specs=(last, last),
        input_output_aliases={2: 0, 3: 1},
        compiler_params=pltpu.CompilerParams(vmem_limit_bytes=16 << 20),
        name="corner",
    )(inner, outer, near, far)


def around(tile_of, v, tile, tiles, west, east, probe, half, variables):
    slot = (probe % (LANES // half // variables)) * variables + v

    def line_up(block, lane):
        return pltpu.roll(block, (lane + LANES - half * slot) % LANES, 1)

    before = tile_of(v, tile - 1) if tile > 0 else line_up(west, LANES - half)
    after = tile_of(v, tile + 1) if tile + 1 < tiles else line_up(east, 0)
    lane = lax.broadcasted_iota(jnp.int32, before.shape, 1)
    return jnp.where(lane < LANES // 2, after, before)


def fold(part):
    height, width = part.shape
    folded = jnp.sum(part.reshape(height // 8, 8, width), axis=0)
    return sum(folded[:, lanes_of(t)] for t in range(width // LANES))


def own_kernel(
    half,
    nugget_ref,
    across_ref,
    downward_ref,
    masked_ref,
    land_ref,
    inner_ref,
    outer_ref,
    out_ref,
    edge_ref,
    sums_ref,
    interior_ref,
):
    probe = pl.program_id(0)
    variables, rows, cols = out_ref.shape[1:]
    kernels = downward_ref.shape[0]
    tiles = cols // LANES
    upper = jnp.where(odd("band"), 0, 1)

    @pl.when(probe == 0)
    def _():
        for first in (0, half + rows):
            blank = (slice(None),) * 3 + (slice(first, first + half), slice(None))
            interior_ref[blank] = jnp.zeros_like(interior_ref[blank])

    group = probe // (LANES // half // variables)
    swapped = odd("region")
    inner, outer = inner_ref[group], outer_ref[group]

    west, east = jnp.where(swapped, inner, outer), jnp.where(swapped, outer, inner)

    def tile_of(v, tile):
        return masked_ref[probe * variables + v, tile]

    sums = [jnp.zeros((8, LANES), F32) for _ in range(kernels + 1)]
    wide = 2 * LANES
    step = downward_ref.shape[1] // variables
    parts = downward_ref.shape[2] // wide

    def filter_columns(chunk):
        for tile in (2 * chunk, 2 * chunk + 1):
            window = []
            for v in range(variables):
                sides = around(tile_of, v, tile, tiles, west, east, probe, half, variables)
                window.append(jnp.concatenate([tile_of(v, tile), sides], axis=1))
            window = jnp.concatenate(window, axis=0)
            both = jnp.dot(window, across_ref[...], preferred_element_type=F32).astype(BF16)
            for kernel in range(kernels):
                interior_ref[kernel, :, tile, half : half + rows] = both[:, lanes_of(kernel)].reshape(
                    variables, rows, LANES
                )

    def filter_rows(chunk):
        span = slice(chunk * wide, (chunk + 1) * wide)
        for first in range(0, rows, step):
            here = slice(first, first + step)
            terms = []
            for kernel in range(kernels):
                window = jnp.concatenate(
                    [
                        interior_ref[kernel, :, tile, first : first + step + 2 * half].reshape(wide, LANES)
                        for tile in (2 * chunk, 2 * chunk + 1)
                    ],
                    axis=1,
                )
                window = jnp.concatenate([window] * parts, axis=0)
                terms.append(jnp.dot(downward_ref[kernel], window, preferred_element_type=F32))
            land = jnp.concatenate([land_ref[2 * chunk, here], land_ref[2 * chunk + 1, here]], axis=1)
            for v in range(variables):
                plane = probe * variables + v
                local = jnp.concatenate(
                    [masked_ref[plane, 2 * chunk, here], masked_ref[plane, 2 * chunk + 1, here]], axis=1
                ).astype(F32)
                total = nugget_ref[v] * local
                sums[kernels] = sums[kernels] + fold(total * local)
                for kernel in range(kernels):
                    term = terms[kernel][v * step : (v + 1) * step]
                    sums[kernel] = sums[kernel] + fold(term * local)
                    total = total + term
                out_ref[0, v, here, span] = total.astype(BF16) * land
                if first == 0:
                    edge_ref[probe, v, upper, :, span] = total[:half]
                if first + step == rows:
                    edge_ref[probe, v, 1 - upper, :, span] = total[step - half :]

    filter_columns(0)
    for chunk in range(cols // wide):
        if chunk + 1 < cols // wide:
            filter_columns(chunk + 1)
        filter_rows(chunk)
    for k in range(kernels + 1):
        sums_ref[probe, k] = sums[k]


def own(nugget, across, downward, masked, land, inner, outer, half, shape):
    count, variables, rows, cols = shape
    kernels = downward.shape[0]
    block = lambda *shape: pl.BlockSpec((1, *shape), lambda p: (p,) + (0,) * len(shape))
    outs = (
        jax.ShapeDtypeStruct(shape, BF16),
        jax.ShapeDtypeStruct((count, variables, 2, half, cols), F32),
        jax.ShapeDtypeStruct((count, kernels + 1, 8, LANES), F32),
    )
    operands = (across, downward, masked, land, inner, outer)
    return pl.pallas_call(
        functools.partial(own_kernel, half),
        grid=(count,),
        out_shape=outs,
        in_specs=[SMEM] + [whole(o) for o in operands],
        out_specs=(block(*shape[1:]), whole(outs[1]), whole(outs[2])),
        scratch_shapes=[pltpu.VMEM((kernels, variables, cols // LANES, rows + 2 * half, LANES), BF16)],
        cost_estimate=pl.CostEstimate(flops=10**10, bytes_accessed=16 << 20, transcendentals=0),
        compiler_params=pltpu.CompilerParams(vmem_limit_bytes=32 << 20),
        name="own",
    )(nugget, *operands)


def border_kernel(
    half,
    across_ref,
    fringe_ref,
    land_ref,
    near_ref,
    far_ref,
    near_own_ref,
    far_own_ref,
    edge_ref,
    sums_ref,
    base_ref,
    out_ref,
    quad_ref,
    ready_ref,
    total_ref,
    sem,
):
    count, variables, _, _, cols = edge_ref.shape
    rows = out_ref.shape[2]
    shares = sums_ref.shape[1]
    kernels = shares - 1
    tiles = cols // LANES
    per_group = LANES // half // variables
    groups = count // per_group
    flipped = odd("region")
    upper = jnp.where(odd("band"), 0, rows - half)
    firsts = [pl.multiple_of(upper, half), pl.multiple_of(rows - half - upper, half)]
    size = 2 * half * variables
    wide = 2 * LANES
    last = count * variables * tiles

    halos = (near_ref, far_ref)

    def corners(ref, p):
        inner, outer = (ref[last + kind + p // per_group] for kind in (0, groups))
        return jnp.where(flipped, inner, outer), jnp.where(flipped, outer, inner)

    ends = {(at, p): corners(halos[at], p) for at in range(2) for p in range(count)}

    def filter_columns(tile):
        window = []
        for p in range(count):
            for v in range(variables):
                for at in range(2):
                    tile_of = lambda v, t: halos[at][(p * variables + v) * tiles + t]
                    sides = around(tile_of, v, tile, tiles, *ends[at, p], p, half, variables)
                    window.append(jnp.concatenate([tile_of(v, tile), sides], axis=1))
        window = jnp.concatenate(window, axis=0)
        both = jnp.dot(window, across_ref[...], preferred_element_type=F32).astype(BF16)
        for kernel in range(kernels):
            piece = both[:, lanes_of(kernel)].reshape(count, size, LANES)
            ready_ref[kernel, :, tile] = piece

    sums = {(p, k): sums_ref[p, k] for p in range(count) for k in range(shares)}

    def filter_rows(chunk):
        span = slice(chunk * wide, (chunk + 1) * wide)
        pair = (2 * chunk, 2 * chunk + 1)
        strips = [
            jnp.concatenate([land_ref[tile, pl.ds(first, half)] for tile in pair], axis=1) for first in firsts
        ]
        shore = jnp.stack(strips)
        for p in range(count):
            near, far = (
                jnp.stack(
                    [
                        jnp.concatenate([ref[(p * variables + v) * tiles + tile] for tile in pair], axis=1)
                        for v in range(variables)
                    ]
                )
                for ref in (near_own_ref, far_own_ref)
            )
            total = edge_ref[p, :, :, :, span]
            local = jnp.stack([near, far], axis=1).astype(F32)
            for kernel in range(kernels):
                window = jnp.concatenate([ready_ref[kernel, p, tile] for tile in pair], axis=1)
                window = jnp.concatenate([window] * (fringe_ref.shape[2] // size), axis=0)
                term = jnp.dot(fringe_ref[kernel], window, preferred_element_type=F32)
                sums[p, kernel] = sums[p, kernel] + fold(term * local.reshape(size, wide))
                total = total + term.reshape(total.shape)
            total_ref[p, :, :, :, span] = total.astype(BF16) * shore[None]

    chunks = cols // wide
    for tile in (0, 1):
        filter_columns(tile)
    for chunk in range(chunks):
        for tile in (2 * chunk + 2, 2 * chunk + 3):
            if tile < tiles:
                filter_columns(tile)
        filter_rows(chunk)

    copies = [
        pltpu.make_async_copy(total_ref.at[:, :, at], out_ref.at[:, :, pl.ds(first, half), :], sem.at[at])
        for at, first in enumerate(firsts)
    ]
    for copy in copies:
        copy.start()

    lane = lax.broadcasted_iota(jnp.int32, quad_ref.shape, 1)
    line = jnp.zeros(quad_ref.shape, F32)
    for (p, k), part in sums.items():
        line = jnp.where(lane == p * shares + k, jnp.sum(part), line)
    quad_ref[...] = line
    for copy in copies:
        copy.wait()


def border(across, fringe, land, near, far, near_own, far_own, edge, sums, base, half, devices):
    count, variables, _, cols = base.shape
    kernels = fringe.shape[0]
    size = 2 * half * variables
    keep = pl.BlockSpec(memory_space=pl.ANY)
    quads = jax.ShapeDtypeStruct((devices, LANES), F32)
    operands = (across, fringe, land, near, far, near_own, far_own, edge, sums)
    return pl.pallas_call(
        functools.partial(border_kernel, half),
        grid=(1,),
        out_shape=(jax.ShapeDtypeStruct(base.shape, BF16), quads),
        in_specs=[whole(o) for o in operands] + [keep],
        out_specs=(keep, whole(quads)),
        scratch_shapes=[
            pltpu.VMEM((kernels, count, cols // LANES, size, LANES), BF16),
            pltpu.VMEM((count, variables, 2, half, cols), BF16),
            pltpu.SemaphoreType.DMA((2,)),
        ],
        input_output_aliases={len(operands): 0},
        compiler_params=pltpu.CompilerParams(vmem_limit_bytes=32 << 20),
        name="border",
    )(*operands, base)


def per_device(probes, filter_taps, mixing, nugget, land_span):
    count, _, rows, cols = probes.shape
    kernels = filter_taps.shape[0]
    half = filter_taps.shape[2] - 1
    regions, bands = lax.axis_size("region"), lax.axis_size("band")
    inner_pairs = [(i, i ^ 1) for i in range(regions)]
    outer_pairs = [(i, (i + 1 if i % 2 else i - 1) % regions) for i in range(regions)]
    near_pairs = [(i, i ^ 1) for i in range(bands)]
    far_pairs = [(i, i + 1 if i % 2 else i - 1) for i in range(1, bands - 1)]

    probes = pltpu.with_memory_space_constraint(probes, pltpu.HBM)
    span = pltpu.with_memory_space_constraint(land_span.reshape(2, 1, rows), pltpu.HBM)
    inner, outer = pack(probes, span, half)
    outer = lax.ppermute(outer, "region", outer_pairs)
    inner = lax.ppermute(inner, "region", inner_pairs)
    masked, near, far, land, across, downward, fringe = prepare(probes, filter_taps, mixing, span, half)
    near, far = corner(inner, outer, near, far)
    near_halo = lax.ppermute(near, "band", near_pairs)
    far_halo = lax.ppermute(far, "band", far_pairs)
    base, edge, sums = own(nugget, across, downward, masked, land, inner, outer, half, probes.shape)
    output, quads = border(
        across, fringe, land, near_halo, far_halo, near, far, edge, sums, base, half, regions * bands
    )
    shares = lax.all_to_all(quads, ("region", "band"), 0, 0, tiled=True)
    quadratic = jnp.sum(shares, axis=0)[: count * (kernels + 1)].reshape(count, kernels + 1)
    return output, quadratic / (bands * rows * cols)


def solution(mesh):
    in_specs = (P(None, None, "band", "region"), P(), P(), P(), P(None, "band", "region"))
    out_specs = (P(None, None, "band", "region"), P())
    return jax.shard_map(
        per_device, mesh=mesh, in_specs=in_specs, out_specs=out_specs, check_vma=False
    )
```
